128 devices in a mesh: row: 8 (over x, core), col: 16 (over z, y).
Axes of the slice: x: 4, y: 4, z: 4, core: 2. Of those that a mesh axis runs over, the one named last changes fastest.
Arguments:
- raw_vectors: float32 [4096, 81920], P('col', 'row'), may hold values from -810 to 810
- interval_count: int32 [16], replicated, may hold values from 1 to 256, 2048 in all
- cluster_of: int32 [16, 256], P('col'), may hold values from 0 to 31, never falling along the last dimension, each value on 1 to 32 neighbouring positions
- panel_one: float32 [81920, 256], P(('row', 'col')), may hold values from -0.03125 to 0.03125
- factor_one: float32 [256, 256], replicated, may hold values from -0.3 to 2
- panel_two: float32 [81920, 256], P(('row', 'col')), may hold values from -0.03125 to 0.03125
- factor_two: float32 [256, 256], replicated, may hold values from -0.3 to 2
Outputs:
- eigenvectors: float32 [2048, 81920], P('col', 'row')
The draws below stay inside these ranges and needn't reach their ends.
Inputs may be any that keep to these rules, and one draw needn't show every extreme that they name: `interval_count`: the counts sum to 2048; one is exactly 256. `cluster_of`: labels never fall along an interval's slots; one label covers at most 32 slots, and one covers exactly 32.
All inputs are finite; a program needn't handle non-finite values.
Results may differ from the reference program's by a relative error of at most 0.0003.
Values sent between devices are 32-bit elements; how exact they have to be, the bound alone decides.
A program may use at most 128 MiB of HBM per device.

```python
import math
import jax
import jax.numpy as jnp
import numpy as np
from jax import lax

N = 81920
R = 256
NB = 16
KD = 128
CAP = 256
K = 2048
SLOTS = 4096
CLUSTERS = 32
CMAX = 32
N_COL = 16


def draw_raw_vectors(key, part):
    key = jax.random.fold_in(key, 13)
    base_key, scale_key, row_key = jax.random.split(key, 3)
    base = jnp.clip(jax.random.normal(base_key, (SLOTS + 1, N), jnp.float32), -6.0, 6.0)
    slot_scale = jnp.exp(jax.random.uniform(scale_key, (SLOTS, 1), jnp.float32, 0.0, math.log(10.0)))
    rising = 1.0 + 2.0 * jnp.arange(N, dtype=jnp.float32)[None, :] / N
    row_scale = jnp.exp(jax.random.uniform(row_key, (1, N), jnp.float32, 0.0, math.log(3.0))) * rising
    return slot_scale * row_scale * (base[:-1] + 0.5 * base[1:])


def draw_factor_one(key, part):
    key = jax.random.fold_in(key, 21)
    diag_key, upper_key = jax.random.split(key, 2)
    diag_values = jax.random.uniform(diag_key, (R,), jnp.float32, 1.0, 2.0)
    upper_values = jnp.clip(0.05 * jax.random.normal(upper_key, (R, R), jnp.float32), -0.3, 0.3)
    upper = jnp.arange(R)[:, None] < jnp.arange(R)[None, :]
    return jnp.where(upper, upper_values, 0.0) + jnp.diag(diag_values)


def draw_factor_two(key, part):
    key = jax.random.fold_in(key, 22)
    diag_key, upper_key = jax.random.split(key, 2)
    diag_values = jax.random.uniform(diag_key, (R,), jnp.float32, 1.0, 2.0)
    upper_values = jnp.clip(0.05 * jax.random.normal(upper_key, (R, R), jnp.float32), -0.3, 0.3)
    upper = jnp.arange(R)[:, None] < jnp.arange(R)[None, :]
    return jnp.where(upper, upper_values, 0.0) + jnp.diag(diag_values)


def block_levels(stream_key, extent, cuts, least, top_value):
    level, own = 1.0, jax.random.fold_in(stream_key, 6)
    for position, shards_of in cuts:
        steps = jnp.exp(jax.random.uniform(jax.random.fold_in(own, position), (shards_of,), jnp.float32, least / len(cuts), top_value / len(cuts)))
        level = level * jnp.repeat(steps, extent[position] // shards_of).reshape([-1 if axis == position else 1 for axis in range(len(extent))])
    return level


def profile(number_of, total, reach, lean):
    weights = [(1 << 20) // math.isqrt(rank ** lean) + 1 for rank in range(2, number_of + 1)]
    surplus, given = total - reach - (number_of - 1), [1] * (number_of - 1)
    while surplus > 0:
        free = [i for i in range(number_of - 1) if given[i] < reach]
        mass, remaining = sum([weights[i] for i in free]), surplus
        for i in free:
            extra = min(reach - given[i], max(1, remaining * weights[i] // mass), surplus)
            given[i] = given[i] + extra
            surplus = surplus - extra
    return np.array([reach] + given)


def ragged(rng, number_of, total, most, slope):
    if number_of == 2:
        one = jax.random.randint(rng, (), max(1, total - most), min(most, total - 1) + 1)
        return jnp.stack([one, total - one])
    tallies = jnp.asarray(profile(number_of, total, most, slope), jnp.int32)
    couples = (number_of - 1) // 2
    source_of, receiver = tallies[1:1 + 2 * couples:2], tallies[2:2 + 2 * couples:2]
    slack = jnp.minimum(source_of - 1, most - receiver)
    moved = jax.random.randint(jax.random.fold_in(rng, 1), (couples,), 0, 1 << 20) % (slack + 1)
    tallies = tallies.at[1:1 + 2 * couples:2].set(source_of - moved).at[2:2 + 2 * couples:2].set(receiver + moved)
    return tallies[jax.random.permutation(jax.random.fold_in(rng, 2), number_of)]


def centred(rng, dims, scale, limit, shards=(), kind=jnp.bfloat16):
    result = scale * jax.random.normal(rng, dims, jnp.float32)
    if shards:
        result = result * block_levels(rng, dims, shards, -0.22, 0.18)
    return jnp.clip(result, -limit, limit).astype(kind)


def setup_inputs(seed: int = 0) -> dict:
    arg_keys = jax.random.split(jax.random.key(seed), 8)
    return {
        "raw_vectors": draw_raw_vectors(jax.random.fold_in(arg_keys[7], 71), 0),
        "interval_count": ragged(arg_keys[1], N_COL, K, CAP, 2).astype(jnp.int32),
        "cluster_of": jax.vmap(lambda own: jnp.searchsorted(jnp.cumsum(ragged(own, CLUSTERS, CAP, CMAX, 2)), jnp.arange(CAP), side="right"))(jax.random.split(arg_keys[2], N_COL)).reshape((N_COL, CAP)).astype(jnp.int32),
        "panel_one": centred(arg_keys[3], (N, R), (N // 2) ** -0.5, 0.03125, ((0, 128),), jnp.float32),
        "factor_one": draw_factor_one(jax.random.fold_in(arg_keys[7], 71), 0),
        "panel_two": centred(arg_keys[5], (N, R), (N // 2) ** -0.5, 0.03125, ((0, 128),), jnp.float32),
        "factor_two": draw_factor_two(jax.random.fold_in(arg_keys[7], 71), 0),
    }


highest = lax.Precision.HIGHEST

def block_order(counts, column_count, per_device, capacity):
    positions = jnp.arange(column_count * per_device, dtype=jnp.int32)
    device_of = positions // per_device
    local_index = positions % per_device
    rank_of = (local_index // NB * column_count + device_of) * NB + local_index % NB
    interval_end = jnp.cumsum(counts).astype(jnp.int32)
    interval_start = interval_end - counts
    owner_device = lax.optimization_barrier(jnp.sum((interval_end[None, :] <= rank_of[:, None]).astype(jnp.int32), axis=1))
    owner_hit = jnp.arange(column_count, dtype=jnp.int32)[None, :] == owner_device[:, None]
    owner_start = lax.optimization_barrier(jnp.sum(jnp.where(owner_hit, interval_start[None, :], 0), axis=1)).astype(jnp.int32)
    return (owner_device * capacity + rank_of - owner_start).astype(jnp.int32)

def finish_block(gram_full, raw_block, labels, is_alive):
    same_group = (labels[:, None] == labels[None, :]) & is_alive[:, None] & is_alive[None, :]
    alive_float = is_alive.astype(jnp.float32)
    masked = jnp.where(same_group, gram_full, 0.0) + jnp.diag(1.0 - alive_float)
    lower_factor = jnp.linalg.cholesky(masked)
    solved = jax.scipy.linalg.solve_triangular(lower_factor, raw_block, lower=True)
    return solved * math.sqrt(N)

def apply_panel(vectors, projected, reflectors, factor):
    scaled = jnp.dot(projected.astype(jnp.float32), factor.T.astype(jnp.float32), precision=highest, preferred_element_type=jnp.float32)
    return vectors - jnp.einsum('kr,nr->kn', scaled, reflectors, precision=highest)

def reference(raw_vectors, interval_count, cluster_of, panel_one, factor_one, panel_two, factor_two):
    blocks = raw_vectors.reshape(N_COL, CAP, N)
    alive_table = jnp.arange(CAP, dtype=jnp.int32)[None, :] < interval_count[:, None]

    def per_interval(members):
        raw_block, labels, is_alive = members
        gram_full = jnp.dot(raw_block.astype(jnp.float32), raw_block.T.astype(jnp.float32), precision=highest, preferred_element_type=jnp.float32)
        return finish_block(gram_full, raw_block, labels, is_alive)
    orthogonal = lax.map(per_interval, (blocks, cluster_of, alive_table)).reshape(SLOTS, N)
    wanted = block_order(interval_count, N_COL, KD, CAP)
    ordered = jnp.take(orthogonal, wanted, axis=0)
    for reflectors, factor in ((panel_two, factor_two), (panel_one, factor_one)):
        projected = jnp.dot(ordered.astype(jnp.float32), reflectors.astype(jnp.float32), precision=highest, preferred_element_type=jnp.float32)
        ordered = apply_panel(ordered, projected, reflectors, factor)
    return ordered
```

```python
import functools
import math

import jax
import jax.numpy as jnp
from jax import lax
from jax.experimental import pallas as pl
from jax.experimental.pallas import tpu as pltpu
from jax.sharding import PartitionSpec as P

N = 81920
CAP = 256
CM = 32
MESH = pl.DeviceIdType.MESH
COLORS = ((0, 192, (0, 1, 2)), (192, 192, (1, 2, 0)), (384, 128, (2, 0, 1)))
HALF = 512

def locate(x, y, z, core):
    return (x * 2 + core, z * 4 + y)

def sum_kernel(x_ref, out_ref, acc, core_in, ring_a, ring_b, plane_in,
               core_s, core_r, ra_s, ra_r, rb_s, rb_r, pl_s, pl_r, gp_s, gp_r, ga_s, ga_r, gb_s, gb_r, gc_s, gc_r):
    row, col = lax.axis_index("row"), lax.axis_index("col")
    core = lax.rem(row, 2)
    at = (lax.div(row, 2), lax.rem(col, 4), lax.div(col, 4))
    partner = locate(at[0], at[1], at[2], 1 - core)

    def along(axis, step):
        moved = list(at)
        moved[axis] = lax.rem(at[axis] + step + 4, 4)
        return locate(moved[0], moved[1], moved[2], core)

    def send(src, dst, s, r, device):
        copy = pltpu.make_async_remote_copy(src, dst, s, r, device_id=device, device_id_type=MESH)
        copy.start()
        return copy

    mine = core * HALF
    other = (1 - core) * HALF
    copies = [send(x_ref.at[pl.ds(other + p * 128, 128)], core_in.at[pl.ds(p * 128, 128)], core_s.at[p], core_r.at[p], partner) for p in range(4)]
    for p in range(4):
        copies[p].wait()
        acc[p * 128:(p + 1) * 128] = x_ref[pl.ds(mine + p * 128, 128)] + core_in[p * 128:(p + 1) * 128]

    def block(color, step):
        base, tiles, order = COLORS[color]
        return base + lax.rem(at[order[0]] + step + 4, 4) * (tiles // 4)

    copies = []
    for color, (base, tiles, order) in enumerate(COLORS):
        size = tiles // 4
        half = size // 2
        far = block(color, 2)
        slot = base // 4
        copies.append(send(acc.at[pl.ds(far, half)], ring_a.at[pl.ds(slot, half)], ra_s.at[color, 0], ra_r.at[color, 0], along(order[0], 1)))
        copies.append(send(acc.at[pl.ds(far + half, half)], ring_a.at[pl.ds(slot + half, half)], ra_s.at[color, 1], ra_r.at[color, 1], along(order[0], -1)))
    for copy in copies:
        copy.wait()
    for color, (base, tiles, order) in enumerate(COLORS):
        size = tiles // 4
        half = size // 2
        slot = base // 4
        after, before = block(color, 1), block(color, -1)
        acc[pl.ds(after, half)] += ring_a[slot:slot + half]
        acc[pl.ds(before + half, half)] += ring_a[slot + half:slot + size]
    copies = []
    for color, (base, tiles, order) in enumerate(COLORS):
        size = tiles // 4
        slot = base // 4
        copies.append(send(acc.at[pl.ds(block(color, 1), size)], ring_b.at[0, pl.ds(slot, size)], rb_s.at[color, 0], rb_r.at[color, 0], along(order[0], 1)))
        copies.append(send(acc.at[pl.ds(block(color, -1), size)], ring_b.at[1, pl.ds(slot, size)], rb_s.at[color, 1], rb_r.at[color, 1], along(order[0], -1)))
    for copy in copies:
        copy.wait()
    for color, (base, tiles, order) in enumerate(COLORS):
        size = tiles // 4
        slot = base // 4
        acc[pl.ds(block(color, 0), size)] += ring_b[0, slot:slot + size] + ring_b[1, slot:slot + size]

    def peer(color, k):
        order = COLORS[color][2]
        moved = list(at)
        moved[order[1]] = lax.rem(at[order[1]] + k % 4, 4)
        moved[order[2]] = lax.rem(at[order[2]] + k // 4, 4)
        return moved[order[2]] * 4 + moved[order[1]], locate(moved[0], moved[1], moved[2], core)

    copies = []
    for k in range(1, 16):
        for color, (base, tiles, order) in enumerate(COLORS):
            piece = tiles // 64
            slot = base // 64
            which, device = peer(color, k)
            copies.append(send(acc.at[pl.ds(block(color, 0) + which * piece, piece)], plane_in.at[k, pl.ds(slot, piece)], pl_s.at[color, k], pl_r.at[color, k], device))
    for copy in copies:
        copy.wait()
    for color, (base, tiles, order) in enumerate(COLORS):
        piece = tiles // 64
        slot = base // 64
        which, _ = peer(color, 0)
        place = block(color, 0) + which * piece
        total = acc[pl.ds(place, piece)]
        for k in range(1, 16):
            total = total + plane_in[k, slot:slot + piece]
        out_ref[pl.ds(mine + place, piece)] = total
    copies = []
    for k in range(1, 16):
        for color, (base, tiles, order) in enumerate(COLORS):
            piece = tiles // 64
            which, _ = peer(color, 0)
            _, device = peer(color, k)
            spot = out_ref.at[pl.ds(mine + block(color, 0) + which * piece, piece)]
            copies.append(send(spot, spot, gp_s.at[color, k], gp_r.at[color, k], device))
    for copy in copies:
        copy.wait()
    copies = []
    for color, (base, tiles, order) in enumerate(COLORS):
        size = tiles // 4
        spot = out_ref.at[pl.ds(mine + block(color, 0), size)]
        copies.append(send(spot, spot, ga_s.at[color, 0], ga_r.at[color, 0], along(order[0], 1)))
        copies.append(send(spot, spot, ga_s.at[color, 1], ga_r.at[color, 1], along(order[0], -1)))
    for copy in copies:
        copy.wait()
    copies = []
    for color, (base, tiles, order) in enumerate(COLORS):
        size = tiles // 4
        half = size // 2
        first = out_ref.at[pl.ds(mine + block(color, -1), half)]
        second = out_ref.at[pl.ds(mine + block(color, 1) + half, half)]
        copies.append(send(first, first, gb_s.at[color, 0], gb_r.at[color, 0], along(order[0], 1)))
        copies.append(send(second, second, gb_s.at[color, 1], gb_r.at[color, 1], along(order[0], -1)))
    for copy in copies:
        copy.wait()
    spot = out_ref.at[pl.ds(mine, HALF)]
    send(spot, spot, gc_s, gc_r, partner).wait()

def sum_all(tiles):
    D = pltpu.SemaphoreType.DMA
    return pl.pallas_call(sum_kernel, out_shape=jax.ShapeDtypeStruct((1024, 8, 128), jnp.float32),
        in_specs=[pl.BlockSpec(memory_space=pltpu.VMEM)], out_specs=pl.BlockSpec(memory_space=pltpu.VMEM),
        scratch_shapes=[pltpu.VMEM((HALF, 8, 128), jnp.float32), pltpu.VMEM((HALF, 8, 128), jnp.float32),
            pltpu.VMEM((128, 8, 128), jnp.float32), pltpu.VMEM((2, 128, 8, 128), jnp.float32), pltpu.VMEM((16, 8, 8, 128), jnp.float32),
            D((4,)), D((4,)), D((3, 2)), D((3, 2)), D((3, 2)), D((3, 2)), D((3, 16)), D((3, 16)), D((3, 16)), D((3, 16)),
            D((3, 2)), D((3, 2)), D((3, 2)), D((3, 2)), D, D],
        compiler_params=pltpu.CompilerParams(has_side_effects=True))(tiles)


def take_lanes(table, index):
    low, high = table[:, :128], table[:, 128:]
    first, second = index[:, :128], index[:, 128:]
    pick = functools.partial(jnp.take_along_axis, axis=1, mode="promise_in_bounds")
    left = pick(low, first)
    right = jnp.where(second >= 128, pick(high, jnp.maximum(second - 128, 0)), pick(low, jnp.minimum(second, 127)))
    return jnp.concatenate([left, right], axis=1)

def factor_kernel(gram_ref, info_ref, out_ref):
    offset = info_ref[0:1, :]
    alive = info_ref[1:2, :]
    window = gram_ref[...]
    for bit, keep in ((7, 160), (6, 96), (5, 64), (4, 48), (3, 40)):
        shift = 1 << bit
        moved = jnp.concatenate([window[shift:], window[:shift]], axis=0)[:keep]
        window = jnp.where(((offset >> bit) & 1) == 1, moved, window[:keep])
    for bit in (2, 1, 0):
        moved = pltpu.roll(window, 40 - (1 << bit), 0)
        window = jnp.where(((offset >> bit) & 1) == 1, moved, window)
    state = window[:CM]
    lane = lax.broadcasted_iota(jnp.int32, (1, CAP), 1)
    position = lane - offset
    live = alive == 1
    sub = lax.broadcasted_iota(jnp.int32, (CM, CAP), 0)
    for k in range(CM - 1):
        active = (position > k) & live
        index = jnp.broadcast_to(jnp.where(active, offset + k, lane), (CM, CAP))
        pivot_row = take_lanes(state, index)
        pivot = jnp.where(active, pivot_row[k:k + 1], 1.0)
        multiplier = jnp.where(active, state[k:k + 1] / pivot, 0.0)
        updated = jnp.where(sub == k, jnp.where(active, -multiplier, state), state - multiplier * pivot_row)
        state = updated
    spot = jnp.broadcast_to(position, (CM, CAP))
    diagonal = jnp.sum(jnp.where(sub == spot, state, 0.0), axis=0, keepdims=True)
    scale = math.sqrt(N) / jnp.sqrt(jnp.where(live, diagonal, 1.0))
    rows = jnp.where(sub < spot, state, jnp.where(sub == spot, 1.0, 0.0)) * scale
    out_ref[:CM] = jnp.where(live, rows, 0.0)
    out_ref[CM:] = jnp.broadcast_to(offset.astype(jnp.float32), (8, CAP))

def factor_inverse(gram, info):
    return pl.pallas_call(factor_kernel, out_shape=jax.ShapeDtypeStruct((40, CAP), jnp.float32))(gram, info)

def expand_kernel(band_ref, hi_ref, lo_ref):
    offset = band_ref[0, CM:CM + 1, :].astype(jnp.int32)
    wide = jnp.concatenate([band_ref[0, :CM], jnp.zeros((8, CAP), jnp.float32)], axis=0)
    for bit in (0, 1, 2):
        wide = jnp.where(((offset >> bit) & 1) == 1, pltpu.roll(wide, 1 << bit, 0), wide)
    for bit, size in ((3, 48), (4, 64), (5, 96), (6, 160), (7, 256)):
        shift = 1 << bit
        have = wide.shape[0]
        plain = jnp.concatenate([wide, jnp.zeros((size - have, CAP), jnp.float32)], axis=0)
        take = min(have, size - shift)
        parts = [jnp.zeros((shift, CAP), jnp.float32), wide[:take]]
        if size - shift - take:
            parts.append(jnp.zeros((size - shift - take, CAP), jnp.float32))
        wide = jnp.where(((offset >> bit) & 1) == 1, jnp.concatenate(parts, axis=0), plain)
    dense = wide.T
    hi = dense.astype(jnp.bfloat16)
    hi_ref[0] = hi
    lo_ref[0] = (dense - hi.astype(jnp.float32)).astype(jnp.bfloat16)

def expand(bands):
    n = bands.shape[0]
    out = jax.ShapeDtypeStruct((n, CAP, CAP), jnp.bfloat16)
    spec = pl.BlockSpec((1, CAP, CAP), lambda s: (s, 0, 0))
    return pl.pallas_call(expand_kernel, grid=(n,), in_specs=[pl.BlockSpec((1, 40, CAP), lambda s: (s, 0, 0))],
        out_specs=(spec, spec), out_shape=(out, out))(bands)

PREC = lax.Precision.HIGHEST


def split(value):
    hi = value.astype(jnp.bfloat16)
    return hi, (value - hi.astype(jnp.float32)).astype(jnp.bfloat16)


def split_outside(value):
    hi = lax.reduce_precision(value, 8, 7)
    return hi.astype(jnp.bfloat16), (value - hi).astype(jnp.bfloat16)


def dot3(a_hi, a_lo, b_hi, b_lo):
    mul = functools.partial(jnp.dot, preferred_element_type=jnp.float32)
    return mul(a_hi, b_hi) + (mul(a_hi, b_lo) + mul(a_lo, b_hi))


def order_kernel(start_ref, t_hi, t_lo, raw_ref, v_hi, v_lo, ordered_ref, tiles_ref, held):
    step = pl.program_id(0)

    @pl.when(step < 16)
    def _():
        z_hi, z_lo = split(raw_ref[0])
        rows = dot3(t_hi[0], t_lo[0], z_hi, z_lo)
        start = start_ref[jnp.minimum(step, 15)]
        lead = lax.rem(start, 8)
        base = pl.multiple_of(start - lead, 8)
        rows = pltpu.roll(jnp.concatenate([rows, jnp.zeros((8, rows.shape[1]), jnp.float32)], axis=0), lead, 0)
        kept = lax.broadcasted_iota(jnp.int32, (8, rows.shape[1]), 0) < lead
        held[pl.ds(base, 8), :] = jnp.where(kept, held[pl.ds(base, 8), :], rows[:8])
        held[pl.ds(base + 8, CAP), :] = rows[8:]

    @pl.when(step >= 16)
    def _():
        first = pl.multiple_of((step - 16) * 256, 256)
        rows = held[pl.ds(first, 256), :]
        ordered_ref[...] = rows
        r_hi, r_lo = split(rows)
        product = dot3(r_hi, r_lo, v_hi[...], v_lo[...])
        for q in range(4):
            tiles_ref[:, q] = product[:, q * 128:(q + 1) * 128].reshape(32, 8, 128)


def order_rows(starts, t_hi, t_lo, spread, v_hi, v_lo):
    early = lambda s, starts: (jnp.minimum(s, 15), 0, 0)
    late = lambda s: jnp.maximum(s - 16, 0)
    width = spread.shape[2]
    return pl.pallas_call(
        order_kernel,
        grid_spec=pltpu.PrefetchScalarGridSpec(
            num_scalar_prefetch=1,
            grid=(24,),
            in_specs=[
                pl.BlockSpec((1, CAP, CAP), early),
                pl.BlockSpec((1, CAP, CAP), early),
                pl.BlockSpec((1, CAP, width), early),
                pl.BlockSpec((width, 512), lambda s, starts: (0, 0)),
                pl.BlockSpec((width, 512), lambda s, starts: (0, 0)),
            ],
            out_specs=(
                pl.BlockSpec((256, width), lambda s, starts: (late(s), 0)),
                pl.BlockSpec((32, 4, 8, 128), lambda s, starts: (late(s), 0, 0, 0)),
            ),
            scratch_shapes=[pltpu.VMEM((2048 + CAP + 8, width), jnp.float32)],
        ),
        out_shape=(
            jax.ShapeDtypeStruct((2048, width), jnp.float32),
            jax.ShapeDtypeStruct((256, 4, 8, 128), jnp.float32),
        ),
    )(starts, t_hi, t_lo, spread, v_hi, v_lo)


def correct_kernel(ordered_ref, tiles_ref, b_hi, b_lo, out_ref):
    parts = [tiles_ref[:, q].reshape(256, 128) for q in range(4)]
    x_hi, x_lo = split(jnp.concatenate(parts, axis=1))
    result = ordered_ref[...] - dot3(x_hi, x_lo, b_hi[...], b_lo[...])
    out_ref[...] = result.reshape(out_ref.shape)


def correct_rows(ordered, tiles, b_hi, b_lo):
    width = ordered.shape[1]
    return pl.pallas_call(
        correct_kernel,
        grid=(8,),
        in_specs=[
            pl.BlockSpec((256, width), lambda k: (k, 0)),
            pl.BlockSpec((32, 4, 8, 128), lambda k: (k, 0, 0, 0)),
            pl.BlockSpec((512, width), lambda k: (0, 0)),
            pl.BlockSpec((512, width), lambda k: (0, 0)),
        ],
        out_specs=pl.BlockSpec((16, 16, width), lambda k: (0, k, 0)),
        out_shape=jax.ShapeDtypeStruct((16, 128, width), jnp.float32),
    )(ordered, tiles, b_hi, b_lo)


def body(raw_vectors, interval_count, cluster_of, panel_one, factor_one, panel_two, factor_two):
    own = lax.axis_index("col")
    spread = lax.all_to_all(raw_vectors, "col", split_axis=1, concat_axis=0, tiled=True)
    width = spread.shape[1]
    gram = lax.psum(
        jnp.dot(raw_vectors, raw_vectors.T, precision=lax.Precision.HIGH, preferred_element_type=jnp.float32), "row"
    )
    starts = jnp.cumsum(interval_count) - interval_count
    own_count = jnp.sum(jnp.where(jnp.arange(16, dtype=jnp.int32) == own, interval_count, 0))
    slots = jnp.arange(CAP, dtype=jnp.int32)
    labels = cluster_of[0]
    offsets = jnp.sum((labels[None, :] < labels[:, None]).astype(jnp.int32), axis=1)
    info = jnp.stack([offsets, (slots < own_count).astype(jnp.int32)])
    bands = lax.all_gather(factor_inverse(gram, info), "col", axis=0)
    t_hi, t_lo = expand(bands)
    both = jnp.concatenate([panel_two, panel_one], axis=1)
    cross = lax.psum(jnp.dot(panel_two.T, panel_one, precision=PREC), ("row", "col"))
    mul = functools.partial(jnp.dot, precision=PREC)
    one = mul(factor_one.T, panel_one.T)
    two = mul(factor_two.T, panel_two.T - mul(cross, one))
    b_hi, b_lo = split_outside(jnp.concatenate([two, one], axis=0))
    v_hi, v_lo = split_outside(both)
    ordered, tiles = order_rows(starts, t_hi, t_lo, spread.reshape(16, CAP, width), v_hi, v_lo)
    tiles = sum_all(tiles.reshape(1024, 8, 128)).reshape(256, 4, 8, 128)
    blocks = correct_rows(ordered, tiles, b_hi, b_lo)
    return lax.all_to_all(blocks.reshape(2048, width), "col", split_axis=0, concat_axis=1, tiled=True)


def solution(mesh):
    placed = (
        P("col", "row"),
        P(),
        P("col", None),
        P(("row", "col"), None),
        P(),
        P(("row", "col"), None),
        P(),
    )
    return jax.shard_map(
        body, mesh=mesh, in_specs=placed, out_specs=P("col", "row"), check_vma=False
    )
```

```python
import functools
import math

import jax
import jax.numpy as jnp
from jax import lax
from jax.experimental import pallas as pl
from jax.experimental.pallas import tpu as pltpu
from jax.sharding import PartitionSpec as P

N = 81920
CAP = 256
CM = 32
TALL = 272
MESH = pl.DeviceIdType.MESH


def split(value):
    hi = value.astype(jnp.bfloat16)
    return hi, (value - hi.astype(jnp.float32)).astype(jnp.bfloat16)


def dot3(a_hi, a_lo, b_hi, b_lo):
    mul = functools.partial(jnp.dot, preferred_element_type=jnp.float32)
    return mul(a_hi, b_hi) + (mul(a_hi, b_lo) + mul(a_lo, b_hi))


CHUNKS = 8


def back_transform_kernel(
    ordered_rows, v_hi, v_lo, b_hi, b_lo, out,
    part, core_in, acc, ring_a, ring_b, plane_in, whole, result,
    core_s, core_r, ra_s, ra_r, rb_s, rb_r, ps_s, ps_r, pg_s, pg_r, ga_s, ga_r, gb_s, gb_r, gc_s, gc_r,
    move_s, move_r, own_sem,
):
    row, col = lax.axis_index("row"), lax.axis_index("col")
    core, x = lax.rem(row, 2), lax.div(row, 2)
    width = ordered_rows.shape[1]
    partner = (x * 2 + 1 - core, col)
    right = (lax.rem(x + 1, 4) * 2 + core, col)
    left = (lax.rem(x + 3, 4) * 2 + core, col)
    mine, other = core * 16, (1 - core) * 16
    here = x * 4
    after, before, far = lax.rem(x + 1, 4) * 4, lax.rem(x + 3, 4) * 4, lax.rem(x + 2, 4) * 4

    remote = functools.partial(pltpu.make_async_remote_copy, device_id_type=MESH)

    barrier = pltpu.get_barrier_semaphore()

    def greet(device):
        pl.semaphore_signal(barrier, 1, device_id=device, device_id_type=MESH)

    for device in (partner, right, left):
        greet(device)

    def greet_column(k, carry):
        greet((row, lax.rem(col + k, 16)))
        return carry

    lax.fori_loop(1, 16, greet_column, 0)
    pl.semaphore_wait(barrier, 18)

    def core_copy(c):
        return remote(part.at[c, pl.ds(other, 16)], core_in.at[c], core_s.at[c], core_r.at[c], device_id=partner)

    def ring_a_copies(c):
        return (
            remote(acc.at[c, pl.ds(far, 2)], ring_a.at[c, pl.ds(0, 2)], ra_s.at[c, 0], ra_r.at[c, 0], device_id=right),
            remote(acc.at[c, pl.ds(far + 2, 2)], ring_a.at[c, pl.ds(2, 2)], ra_s.at[c, 1], ra_r.at[c, 1], device_id=left),
        )

    def ring_b_copies(c):
        return (
            remote(acc.at[c, pl.ds(after, 4)], ring_b.at[c, 0], rb_s.at[c, 0], rb_r.at[c, 0], device_id=right),
            remote(acc.at[c, pl.ds(before, 4)], ring_b.at[c, 1], rb_s.at[c, 1], rb_r.at[c, 1], device_id=left),
        )

    def plane_copy(c, k):
        peer = lax.rem(col + k, 16)
        source = acc.at[c, here + lax.div(peer, 4), lax.rem(peer, 4)]
        return remote(source, plane_in.at[c, k], ps_s.at[c, k], ps_r.at[c, k], device_id=(row, peer))

    def gather_copy(c, k):
        spot = whole.at[c, mine + here + lax.div(col, 4), lax.rem(col, 4)]
        return remote(spot, spot, pg_s.at[c, k], pg_r.at[c, k], device_id=(row, lax.rem(col + k, 16)))

    def spread_copies(c):
        spot = whole.at[c, pl.ds(mine + here, 4)]
        return (
            remote(spot, spot, ga_s.at[c, 0], ga_r.at[c, 0], device_id=right),
            remote(spot, spot, ga_s.at[c, 1], ga_r.at[c, 1], device_id=left),
        )

    def forward_copies(c):
        first, second = whole.at[c, pl.ds(mine + before, 2)], whole.at[c, pl.ds(mine + after + 2, 2)]
        return (
            remote(first, first, gb_s.at[c, 0], gb_r.at[c, 0], device_id=right),
            remote(second, second, gb_s.at[c, 1], gb_r.at[c, 1], device_id=left),
        )

    def share_copy(c):
        spot = whole.at[c, pl.ds(mine, 16)]
        return remote(spot, spot, gc_s.at[c], gc_r.at[c], device_id=partner)

    def window(c, source):
        return out.at[pl.ds(pl.multiple_of(c * 16, 16), 16), pl.ds(pl.multiple_of(source * width, 128), width)]

    def slab(c, target):
        return result.at[c, pl.ds(pl.multiple_of(target * 16, 16), 16)]

    def move_copy(c, k):
        target = lax.rem(col + k, 16)
        return remote(slab(c, target), window(c, col), move_s.at[c, k], move_r.at[c, k], device_id=(row, target))

    def own_copy(c):
        return pltpu.make_async_copy(slab(c, col), window(c, col), own_sem.at[c])

    def start(*copies):
        for copy in copies:
            copy.start()

    def wait(*copies):
        for copy in copies:
            copy.wait()

    def each(first, last, action):
        def step(k, carry):
            action(k)
            return carry
        lax.fori_loop(first, last, step, 0)

    def ordered(c):
        return ordered_rows[pl.ds(pl.multiple_of(c * 256, 256), 256), :]

    def project(c):
        r_hi, r_lo = split(ordered(c))
        product = dot3(r_hi, r_lo, v_hi[...], v_lo[...])
        for q in range(4):
            part[c, :, q] = product[:, q * 128:(q + 1) * 128].reshape(32, 8, 128)
        start(core_copy(c))

    def fold_core(c):
        wait(core_copy(c))
        acc[c] = part[c, pl.ds(mine, 16)] + core_in[c]
        start(*ring_a_copies(c))

    def fold_a(c):
        wait(*ring_a_copies(c))
        acc[c, pl.ds(after, 2)] += ring_a[c, 0:2]
        acc[c, pl.ds(before + 2, 2)] += ring_a[c, 2:4]
        start(*ring_b_copies(c))

    def fold_b(c):
        wait(*ring_b_copies(c))
        acc[c, pl.ds(here, 4)] += ring_b[c, 0] + ring_b[c, 1]
        each(1, 16, lambda k: plane_copy(c, k).start())

    def fold_plane(c):
        each(1, 16, lambda k: plane_copy(c, k).wait())
        total = acc[c, here + lax.div(col, 4), lax.rem(col, 4)]
        for k in range(1, 16):
            total = total + plane_in[c, k]
        whole[c, mine + here + lax.div(col, 4), lax.rem(col, 4)] = total
        each(1, 16, lambda k: gather_copy(c, k).start())

    def gather_plane(c):
        each(1, 16, lambda k: gather_copy(c, k).wait())
        start(*spread_copies(c))

    def forward(c):
        wait(*spread_copies(c))
        start(*forward_copies(c))

    def share(c):
        wait(*forward_copies(c))
        start(share_copy(c))

    def correct(c):
        wait(share_copy(c))
        x_hi, x_lo = split(jnp.concatenate([whole[c, :, q].reshape(256, 128) for q in range(4)], axis=1))
        result[c] = ordered(c) - dot3(x_hi, x_lo, b_hi[...], b_lo[...])
        each(1, 16, lambda k: move_copy(c, k).start())
        own_copy(c).start()

    stages = (
        (1, fold_core), (2, fold_a), (3, fold_b), (5, fold_plane), (7, gather_plane), (8, forward), (9, share),
        (10, correct), (0, project),
    )

    def tick(t, carry):
        for lag, stage in stages:
            c = t - lag

            @pl.when((c >= 0) & (c < CHUNKS))
            def _(stage=stage, c=c):
                stage(c)

        return carry

    lax.fori_loop(0, CHUNKS + 10, tick, 0)

    def finish(c):
        each(1, 16, lambda k: move_copy(c, k).wait())
        own_copy(c).wait()

    each(0, CHUNKS, finish)


def back_transform(ordered, v_hi, v_lo, b_hi, b_lo):
    width = v_hi.shape[0]
    D, V = pltpu.SemaphoreType.DMA, pltpu.VMEM
    pair = [D((CHUNKS, 2)), D((CHUNKS, 2))]
    many = [D((CHUNKS, 16)), D((CHUNKS, 16))]
    one = [D((CHUNKS,)), D((CHUNKS,))]
    tile = lambda *lead: V((*lead, 8, 128), jnp.float32)
    return pl.pallas_call(
        back_transform_kernel,
        out_shape=jax.ShapeDtypeStruct((128, 16 * width), jnp.float32),
        in_specs=[pl.BlockSpec(memory_space=pltpu.VMEM)] * 5,
        out_specs=pl.BlockSpec(memory_space=pl.ANY),
        scratch_shapes=[
            tile(CHUNKS, 32, 4), tile(CHUNKS, 16, 4), tile(CHUNKS, 16, 4), tile(CHUNKS, 4, 4), tile(CHUNKS, 2, 4, 4),
            tile(CHUNKS, 16), tile(CHUNKS, 32, 4), V((CHUNKS, 256, width), jnp.float32),
            *one, *pair, *pair, *many, *many, *pair, *pair, *one, *many, D((CHUNKS,)),
        ],
        compiler_params=pltpu.CompilerParams(collective_id=7, has_side_effects=True, vmem_limit_bytes=60 * 1024 * 1024),
    )(ordered, v_hi, v_lo, b_hi, b_lo)


def take_lanes(table, index):
    low, high = table[:, :128], table[:, 128:]
    first, second = index[:, :128], index[:, 128:]
    pick = functools.partial(jnp.take_along_axis, axis=1, mode="promise_in_bounds")
    left = pick(low, first)
    right = jnp.where(second >= 128, pick(high, jnp.maximum(second - 128, 0)), pick(low, jnp.minimum(second, 127)))
    return jnp.concatenate([left, right], axis=1)

def factor_kernel(gram_ref, info_ref, out_ref):
    offset = info_ref[0:1, :]
    alive = info_ref[1:2, :]
    window = gram_ref[...]
    for bit, keep in ((7, 160), (6, 96), (5, 64), (4, 48), (3, 40)):
        shift = 1 << bit
        moved = jnp.concatenate([window[shift:], window[:shift]], axis=0)[:keep]
        window = jnp.where(((offset >> bit) & 1) == 1, moved, window[:keep])
    for bit in (2, 1, 0):
        moved = pltpu.roll(window, 40 - (1 << bit), 0)
        window = jnp.where(((offset >> bit) & 1) == 1, moved, window)
    state = window[:CM]
    lane = lax.broadcasted_iota(jnp.int32, (1, CAP), 1)
    position = lane - offset
    live = alive == 1
    sub = lax.broadcasted_iota(jnp.int32, (CM, CAP), 0)
    for k in range(CM - 1):
        active = (position > k) & live
        index = jnp.broadcast_to(jnp.where(active, offset + k, lane), (CM, CAP))
        pivot_row = take_lanes(state, index)
        pivot = jnp.where(active, pivot_row[k:k + 1], 1.0)
        multiplier = jnp.where(active, state[k:k + 1] / pivot, 0.0)
        updated = jnp.where(sub == k, jnp.where(active, -multiplier, state), state - multiplier * pivot_row)
        state = updated
    spot = jnp.broadcast_to(position, (CM, CAP))
    diagonal = jnp.sum(jnp.where(sub == spot, state, 0.0), axis=0, keepdims=True)
    scale = math.sqrt(N) / jnp.sqrt(jnp.where(live, diagonal, 1.0))
    rows = jnp.where(sub < spot, state, jnp.where(sub == spot, 1.0, 0.0)) * scale
    out_ref[:CM] = jnp.where(live, rows, 0.0)
    out_ref[CM:] = jnp.broadcast_to(offset.astype(jnp.float32), (8, CAP))

def factor_inverse(gram, info):
    return pl.pallas_call(factor_kernel, out_shape=jax.ShapeDtypeStruct((40, CAP), jnp.float32))(gram, info)

def expand_kernel(start_ref, band_ref, hi_ref, lo_ref):
    lead = lax.rem(start_ref[pl.program_id(0)], 8)
    offset = band_ref[0, CM:CM + 1, :].astype(jnp.int32)
    wide = jnp.concatenate([band_ref[0, :CM], jnp.zeros((8, CAP), jnp.float32)], axis=0)
    for bit in (0, 1, 2):
        wide = jnp.where(((offset >> bit) & 1) == 1, pltpu.roll(wide, 1 << bit, 0), wide)
    for bit, size in ((3, 48), (4, 64), (5, 96), (6, 160), (7, 256)):
        shift = 1 << bit
        have = wide.shape[0]
        plain = jnp.concatenate([wide, jnp.zeros((size - have, CAP), jnp.float32)], axis=0)
        take = min(have, size - shift)
        parts = [jnp.zeros((shift, CAP), jnp.float32), wide[:take]]
        if size - shift - take:
            parts.append(jnp.zeros((size - shift - take, CAP), jnp.float32))
        wide = jnp.where(((offset >> bit) & 1) == 1, jnp.concatenate(parts, axis=0), plain)
    dense = jnp.concatenate([wide.T, jnp.zeros((TALL - CAP, CAP), jnp.float32)], axis=0)
    hi, lo = split(pltpu.roll(dense, lead, 0))
    hi_ref[0] = hi
    lo_ref[0] = lo


def expand(starts, bands):
    out = jax.ShapeDtypeStruct((16, TALL, CAP), jnp.bfloat16)
    spec = pl.BlockSpec((1, TALL, CAP), lambda s, starts: (s, 0, 0))
    return pl.pallas_call(
        expand_kernel,
        grid_spec=pltpu.PrefetchScalarGridSpec(
            num_scalar_prefetch=1,
            grid=(16,),
            in_specs=[pl.BlockSpec((1, 40, CAP), lambda s, starts: (s, 0, 0))],
            out_specs=(spec, spec),
        ),
        out_shape=(out, out),
    )(starts, bands)


def order_kernel(start_ref, t_hi, t_lo, raw_ref, held):
    start = start_ref[pl.program_id(0)]
    lead = lax.rem(start, 8)
    base = pl.multiple_of(start - lead, 8)
    z_hi, z_lo = split(raw_ref[0])
    rows = dot3(t_hi[0], t_lo[0], z_hi, z_lo)
    kept = lax.broadcasted_iota(jnp.int32, (8, rows.shape[1]), 0) < lead
    held[pl.ds(base, 8), :] = jnp.where(kept, held[pl.ds(base, 8), :], rows[:8])
    held[pl.ds(base + 8, CAP), :] = rows[8:CAP + 8]


def order_rows(starts, t_hi, t_lo, spread):
    width = spread.shape[2]
    factor = pl.BlockSpec((1, TALL, CAP), lambda s, starts: (s, 0, 0))
    return pl.pallas_call(
        order_kernel,
        grid_spec=pltpu.PrefetchScalarGridSpec(
            num_scalar_prefetch=1,
            grid=(16,),
            in_specs=[factor, factor, pl.BlockSpec((1, CAP, width), lambda s, starts: (s, 0, 0))],
            out_specs=pl.BlockSpec((2048 + CAP + 8, width), lambda s, starts: (0, 0)),
        ),
        out_shape=jax.ShapeDtypeStruct((2048 + CAP + 8, width), jnp.float32),
    )(starts, t_hi, t_lo, spread)


def sums_kernel(gram, cross, gram_out, cross_out, gram_in, cross_in, cross_mine, cross_all, s1, r1, s2, r2, s3, r3, s4, r4, s5, r5):
    row, col = lax.axis_index("row"), lax.axis_index("col")
    remote = functools.partial(pltpu.make_async_remote_copy, device_id_type=MESH)
    rows = lambda r: pl.ds(pl.multiple_of(r * 32, 32), 32)
    first, second, third = [], [], []
    for k in range(1, 8):
        peer = lax.rem(row + k, 8)
        first.append(remote(gram.at[rows(peer)], gram_in.at[k], s1.at[k], r1.at[k], device_id=(peer, col)))
        first.append(remote(cross.at[rows(peer)], cross_in.at[k], s2.at[k], r2.at[k], device_id=(peer, col)))
    for copy in first:
        copy.start()
    for copy in first:
        copy.wait()
    gram_sum, cross_sum = gram[rows(row)], cross[rows(row)]
    for k in range(1, 8):
        gram_sum = gram_sum + gram_in[k]
        cross_sum = cross_sum + cross_in[k]
    gram_out[rows(row)] = gram_sum
    cross_mine[...] = cross_sum
    for k in range(1, 16):
        peer = lax.rem(col + k, 16)
        second.append(remote(cross_mine, cross_all.at[k], s3.at[k], r3.at[k], device_id=(row, peer)))
    for k in range(1, 8):
        peer = lax.rem(row + k, 8)
        second.append(remote(gram_out.at[rows(row)], gram_out.at[rows(row)], s4.at[k], r4.at[k], device_id=(peer, col)))
    for copy in second:
        copy.start()
    for copy in second:
        copy.wait()
    for k in range(1, 16):
        cross_sum = cross_sum + cross_all[k]
    cross_out[rows(row)] = cross_sum
    for k in range(1, 8):
        peer = lax.rem(row + k, 8)
        third.append(remote(cross_out.at[rows(row)], cross_out.at[rows(row)], s5.at[k], r5.at[k], device_id=(peer, col)))
    for copy in third:
        copy.start()
    for copy in third:
        copy.wait()


def small_sums(gram, cross):
    D, V = pltpu.SemaphoreType.DMA, pltpu.VMEM
    out = jax.ShapeDtypeStruct((CAP, CAP), jnp.float32)
    vmem = pl.BlockSpec(memory_space=pltpu.VMEM)
    return pl.pallas_call(
        sums_kernel,
        out_shape=(out, out),
        in_specs=[vmem, vmem],
        out_specs=(vmem, vmem),
        scratch_shapes=[
            V((8, 32, CAP), jnp.float32), V((8, 32, CAP), jnp.float32), V((32, CAP), jnp.float32), V((16, 32, CAP), jnp.float32),
            D((8,)), D((8,)), D((8,)), D((8,)), D((16,)), D((16,)), D((8,)), D((8,)), D((8,)), D((8,)),
        ],
        compiler_params=pltpu.CompilerParams(has_side_effects=True),
    )(gram, cross)


def gather_kernel(band, out, s, r):
    row, col = lax.axis_index("row"), lax.axis_index("col")
    copies = []
    for k in range(1, 16):
        peer = lax.rem(col + k, 16)
        copies.append(
            pltpu.make_async_remote_copy(band, out.at[col], s.at[k], r.at[k], device_id=(row, peer), device_id_type=MESH)
        )
    for copy in copies:
        copy.start()
    out[col] = band[...]
    for copy in copies:
        copy.wait()


def gather_bands(band):
    D = pltpu.SemaphoreType.DMA
    vmem = pl.BlockSpec(memory_space=pltpu.VMEM)
    return pl.pallas_call(
        gather_kernel,
        out_shape=jax.ShapeDtypeStruct((16, *band.shape), jnp.float32),
        in_specs=[vmem],
        out_specs=vmem,
        scratch_shapes=[D((16,)), D((16,))],
        compiler_params=pltpu.CompilerParams(has_side_effects=True),
    )(band)


def by_target_kernel(raw, out):
    out[0] = raw[...]


def by_target(raw, width):
    rows = raw.shape[0]
    return pl.pallas_call(
        by_target_kernel,
        grid=(16,),
        in_specs=[pl.BlockSpec((rows, width), lambda t: (0, t))],
        out_specs=pl.BlockSpec((1, rows, width), lambda t: (t, 0, 0)),
        out_shape=jax.ShapeDtypeStruct((16, rows, width), jnp.float32),
    )(raw)


def split_outside(value):
    hi = lax.reduce_precision(value, 8, 7)
    return hi.astype(jnp.bfloat16), (value - hi).astype(jnp.bfloat16)


def body(raw_vectors, interval_count, cluster_of, panel_one, factor_one, panel_two, factor_two):
    own = lax.axis_index("col")
    width = raw_vectors.shape[1] // 16
    spread = lax.all_to_all(by_target(raw_vectors, width), "col", split_axis=0, concat_axis=0)
    mul = functools.partial(jnp.dot, precision=lax.Precision.HIGHEST)
    gram_part = jnp.dot(
        raw_vectors, raw_vectors.T, precision=lax.Precision.HIGH, preferred_element_type=jnp.float32
    )
    gram, cross = small_sums(gram_part, mul(panel_two.T, panel_one))
    starts = jnp.cumsum(interval_count) - interval_count
    own_count = jnp.sum(jnp.where(jnp.arange(16, dtype=jnp.int32) == own, interval_count, 0))
    slots = jnp.arange(CAP, dtype=jnp.int32)
    labels = cluster_of[0]
    offsets = jnp.sum((labels[None, :] < labels[:, None]).astype(jnp.int32), axis=1)
    info = jnp.stack([offsets, (slots < own_count).astype(jnp.int32)])
    t_hi, t_lo = expand(starts, gather_bands(factor_inverse(gram, info)))
    one = mul(factor_one.T, panel_one.T)
    two = mul(factor_two.T, panel_two.T - mul(cross, one))
    b_hi, b_lo = split_outside(jnp.concatenate([two, one], axis=0))
    v_hi, v_lo = split_outside(jnp.concatenate([panel_two, panel_one], axis=1))
    ordered = order_rows(starts, t_hi, t_lo, spread)
    return back_transform(ordered, v_hi, v_lo, b_hi, b_lo)


def solution(mesh):
    placed = (
        P("col", "row"),
        P(),
        P("col", None),
        P(("row", "col"), None),
        P(),
        P(("row", "col"), None),
        P(),
    )
    return jax.shard_map(
        body, mesh=mesh, in_specs=placed, out_specs=P("col", "row"), check_vma=False
    )
```

```python
import functools
import math

import jax
import jax.numpy as jnp
from jax import lax
from jax.experimental import pallas as pl
from jax.experimental.pallas import tpu as pltpu
from jax.sharding import PartitionSpec as P

N = 81920
CAP = 256
CM = 32
TALL = 272
MESH = pl.DeviceIdType.MESH


def split(value):
    hi = value.astype(jnp.bfloat16)
    return hi, (value - hi.astype(jnp.float32)).astype(jnp.bfloat16)


def dot3(a_hi, a_lo, b_hi, b_lo):
    mul = functools.partial(jnp.dot, preferred_element_type=jnp.float32)
    return mul(a_hi, b_hi) + (mul(a_hi, b_lo) + mul(a_lo, b_hi))


CHUNKS = 8


def back_transform_kernel(
    ordered_rows, v_hi, v_lo, b_hi, b_lo, out,
    part, core_in, acc, ring_a, ring_b, plane_in, whole, result,
    core_s, core_r, ra_s, ra_r, rb_s, rb_r, ps_s, ps_r, pg_s, pg_r, ga_s, ga_r, gb_s, gb_r, gc_s, gc_r,
    move_s, move_r, own_sem,
):
    row, col = lax.axis_index("row"), lax.axis_index("col")
    core, x = lax.rem(row, 2), lax.div(row, 2)
    width = ordered_rows.shape[1]
    partner = (x * 2 + 1 - core, col)
    right = (lax.rem(x + 1, 4) * 2 + core, col)
    left = (lax.rem(x + 3, 4) * 2 + core, col)
    mine, other = core * 16, (1 - core) * 16
    here = x * 4
    after, before, far = lax.rem(x + 1, 4) * 4, lax.rem(x + 3, 4) * 4, lax.rem(x + 2, 4) * 4

    remote = functools.partial(pltpu.make_async_remote_copy, device_id_type=MESH)

    barrier = pltpu.get_barrier_semaphore()

    def greet(device):
        pl.semaphore_signal(barrier, 1, device_id=device, device_id_type=MESH)

    for device in (partner, right, left):
        greet(device)

    def greet_column(k, carry):
        greet((row, lax.rem(col + k, 16)))
        return carry

    lax.fori_loop(1, 16, greet_column, 0)
    pl.semaphore_wait(barrier, 18)

    def core_copy(c):
        return remote(part.at[c, pl.ds(other, 16)], core_in.at[c], core_s.at[c], core_r.at[c], device_id=partner)

    def ring_a_copies(c):
        return (
            remote(acc.at[c, pl.ds(far, 2)], ring_a.at[c, pl.ds(0, 2)], ra_s.at[c, 0], ra_r.at[c, 0], device_id=right),
            remote(acc.at[c, pl.ds(far + 2, 2)], ring_a.at[c, pl.ds(2, 2)], ra_s.at[c, 1], ra_r.at[c, 1], device_id=left),
        )

    def ring_b_copies(c):
        return (
            remote(acc.at[c, pl.ds(after, 4)], ring_b.at[c, 0], rb_s.at[c, 0], rb_r.at[c, 0], device_id=right),
            remote(acc.at[c, pl.ds(before, 4)], ring_b.at[c, 1], rb_s.at[c, 1], rb_r.at[c, 1], device_id=left),
        )

    def plane_copy(c, k):
        peer = lax.rem(col + k, 16)
        source = acc.at[c, here + lax.div(peer, 4), lax.rem(peer, 4)]
        return remote(source, plane_in.at[c, k], ps_s.at[c, k], ps_r.at[c, k], device_id=(row, peer))

    def gather_copy(c, k):
        spot = whole.at[c, mine + here + lax.div(col, 4), lax.rem(col, 4)]
        return remote(spot, spot, pg_s.at[c, k], pg_r.at[c, k], device_id=(row, lax.rem(col + k, 16)))

    def spread_copies(c):
        spot = whole.at[c, pl.ds(mine + here, 4)]
        return (
            remote(spot, spot, ga_s.at[c, 0], ga_r.at[c, 0], device_id=right),
            remote(spot, spot, ga_s.at[c, 1], ga_r.at[c, 1], device_id=left),
        )

    def forward_copies(c):
        first, second = whole.at[c, pl.ds(mine + before, 2)], whole.at[c, pl.ds(mine + after + 2, 2)]
        return (
            remote(first, first, gb_s.at[c, 0], gb_r.at[c, 0], device_id=right),
            remote(second, second, gb_s.at[c, 1], gb_r.at[c, 1], device_id=left),
        )

    def share_copy(c):
        spot = whole.at[c, pl.ds(mine, 16)]
        return remote(spot, spot, gc_s.at[c], gc_r.at[c], device_id=partner)

    def window(c, source):
        return out.at[pl.ds(pl.multiple_of(c * 16, 16), 16), pl.ds(pl.multiple_of(source * width, 128), width)]

    def slab(c, target):
        return result.at[c, pl.ds(pl.multiple_of(target * 16, 16), 16)]

    def move_copy(c, k):
        target = lax.rem(col + k, 16)
        return remote(slab(c, target), window(c, col), move_s.at[c, k], move_r.at[c, k], device_id=(row, target))

    def own_copy(c):
        return pltpu.make_async_copy(slab(c, col), window(c, col), own_sem.at[c])

    def start(*copies):
        for copy in copies:
            copy.start()

    def wait(*copies):
        for copy in copies:
            copy.wait()

    def each(first, last, action):
        def step(k, carry):
            action(k)
            return carry
        lax.fori_loop(first, last, step, 0)

    def ordered(c):
        return ordered_rows[pl.ds(pl.multiple_of(c * 256, 256), 256), :]

    def project(c):
        r_hi, r_lo = split(ordered(c))
        product = dot3(r_hi, r_lo, v_hi[...], v_lo[...])
        for q in range(4):
            part[c, :, q] = product[:, q * 128:(q + 1) * 128].reshape(32, 8, 128)
        start(core_copy(c))

    def fold_core(c):
        wait(core_copy(c))
        acc[c] = part[c, pl.ds(mine, 16)] + core_in[c]
        start(*ring_a_copies(c))

    def fold_a(c):
        wait(*ring_a_copies(c))
        acc[c, pl.ds(after, 2)] += ring_a[c, 0:2]
        acc[c, pl.ds(before + 2, 2)] += ring_a[c, 2:4]
        start(*ring_b_copies(c))

    def fold_b(c):
        wait(*ring_b_copies(c))
        acc[c, pl.ds(here, 4)] += ring_b[c, 0] + ring_b[c, 1]
        each(1, 16, lambda k: plane_copy(c, k).start())

    def fold_plane(c):
        each(1, 16, lambda k: plane_copy(c, k).wait())
        total = acc[c, here + lax.div(col, 4), lax.rem(col, 4)]
        for k in range(1, 16):
            total = total + plane_in[c, k]
        whole[c, mine + here + lax.div(col, 4), lax.rem(col, 4)] = total
        each(1, 16, lambda k: gather_copy(c, k).start())

    def gather_plane(c):
        each(1, 16, lambda k: gather_copy(c, k).wait())
        start(*spread_copies(c))

    def forward(c):
        wait(*spread_copies(c))
        start(*forward_copies(c))

    def share(c):
        wait(*forward_copies(c))
        start(share_copy(c))

    def correct(c):
        wait(share_copy(c))
        x_hi, x_lo = split(jnp.concatenate([whole[c, :, q].reshape(256, 128) for q in range(4)], axis=1))
        result[c] = ordered(c) - dot3(x_hi, x_lo, b_hi[...], b_lo[...])
        each(1, 16, lambda k: move_copy(c, k).start())
        own_copy(c).start()

    stages = (
        (1, fold_core), (2, fold_a), (3, fold_b), (5, fold_plane), (7, gather_plane), (8, forward), (9, share),
        (10, correct), (0, project),
    )

    def tick(t, carry):
        for lag, stage in stages:
            c = t - lag

            @pl.when((c >= 0) & (c < CHUNKS))
            def _(stage=stage, c=c):
                stage(c)

        return carry

    lax.fori_loop(0, CHUNKS + 10, tick, 0)

    def finish(c):
        each(1, 16, lambda k: move_copy(c, k).wait())
        own_copy(c).wait()

    each(0, CHUNKS, finish)


def back_transform(ordered, v_hi, v_lo, b_hi, b_lo):
    width = v_hi.shape[0]
    D, V = pltpu.SemaphoreType.DMA, pltpu.VMEM
    pair = [D((CHUNKS, 2)), D((CHUNKS, 2))]
    many = [D((CHUNKS, 16)), D((CHUNKS, 16))]
    one = [D((CHUNKS,)), D((CHUNKS,))]
    tile = lambda *lead: V((*lead, 8, 128), jnp.float32)
    return pl.pallas_call(
        back_transform_kernel,
        out_shape=jax.ShapeDtypeStruct((128, 16 * width), jnp.float32),
        in_specs=[pl.BlockSpec(memory_space=pltpu.VMEM)] * 5,
        out_specs=pl.BlockSpec(memory_space=pl.ANY),
        scratch_shapes=[
            tile(CHUNKS, 32, 4), tile(CHUNKS, 16, 4), tile(CHUNKS, 16, 4), tile(CHUNKS, 4, 4), tile(CHUNKS, 2, 4, 4),
            tile(CHUNKS, 16), tile(CHUNKS, 32, 4), V((CHUNKS, 256, width), jnp.float32),
            *one, *pair, *pair, *many, *many, *pair, *pair, *one, *many, D((CHUNKS,)),
        ],
        compiler_params=pltpu.CompilerParams(collective_id=7, has_side_effects=True, vmem_limit_bytes=60 * 1024 * 1024),
    )(ordered, v_hi, v_lo, b_hi, b_lo)


EARLY = 5
ROWS = CAP // 8


def inverse_band(window, offset, live):
    lane = lax.broadcasted_iota(jnp.int32, (1, CAP), 1)
    position = lane - offset
    sub = lax.broadcasted_iota(jnp.int32, (CM, CAP), 0)
    state = window
    for k in range(CM - 1):
        active = (position > k) & live
        distance = jnp.where(active, position - k, 0)
        pivot_row = state
        for bit in range(5):
            take = jnp.broadcast_to(((distance >> bit) & 1) == 1, (CM, CAP))
            pivot_row = jnp.where(take, pltpu.roll(pivot_row, 1 << bit, 1), pivot_row)
        pivot = jnp.where(active, pivot_row[k:k + 1], 1.0)
        multiplier = jnp.where(active, state[k:k + 1] / pivot, 0.0)
        state = jnp.where(sub == k, jnp.where(active, -multiplier, state), state - multiplier * pivot_row)
    spot = jnp.broadcast_to(position, (CM, CAP))
    diagonal = jnp.sum(jnp.where(sub == spot, state, 0.0), axis=0, keepdims=True)
    scale = math.sqrt(N) / jnp.sqrt(jnp.where(live, diagonal, 1.0))
    rows = jnp.where(sub < spot, state, jnp.where(sub == spot, 1.0, 0.0)) * scale
    return jnp.where(live, rows, 0.0)


def cluster_window(gram, offset):
    window = gram
    for bit, keep in ((7, 160), (6, 96), (5, 64), (4, 48), (3, 40)):
        shift = 1 << bit
        moved = jnp.concatenate([window[shift:], window[:shift]], axis=0)[:keep]
        window = jnp.where(((offset >> bit) & 1) == 1, moved, window[:keep])
    for bit in (2, 1, 0):
        moved = pltpu.roll(window, 40 - (1 << bit), 0)
        window = jnp.where(((offset >> bit) & 1) == 1, moved, window)
    return window[:CM]


def dense_rows(band, offset, lead):
    wide = jnp.concatenate([band, jnp.zeros((8, CAP), jnp.float32)], axis=0)
    for bit in (0, 1, 2):
        wide = jnp.where(((offset >> bit) & 1) == 1, pltpu.roll(wide, 1 << bit, 0), wide)
    for bit, size in ((3, 48), (4, 64), (5, 96), (6, 160), (7, 256)):
        shift = 1 << bit
        have = wide.shape[0]
        plain = jnp.concatenate([wide, jnp.zeros((size - have, CAP), jnp.float32)], axis=0)
        take = min(have, size - shift)
        parts = [jnp.zeros((shift, CAP), jnp.float32), wide[:take]]
        if size - shift - take:
            parts.append(jnp.zeros((size - shift - take, CAP), jnp.float32))
        wide = jnp.where(((offset >> bit) & 1) == 1, jnp.concatenate(parts, axis=0), plain)
    dense = jnp.concatenate([wide.T, jnp.zeros((TALL - CAP, CAP), jnp.float32)], axis=0)
    for bit in range(3):
        dense = jnp.where(((lead >> bit) & 1) == 1, pltpu.roll(dense, 1 << bit, 0), dense)
    return dense


def front_kernel(
    counts, raw, labels, panel_one, factor_one, panel_two, factor_two,
    spread, t_hi, t_lo, v_hi, v_lo, b_hi, b_lo,
    held, gram_high, gram_low, cross, window, window_in, cross_in, cross_mine, cross_all, cross_sum, band, bands,
    load_sem, own_sem, move_s, move_r, win_s, win_r, cr_s, cr_r, ca_s, ca_r, cg_s, cg_r, bd_s, bd_r,
):
    row, col = lax.axis_index("row"), lax.axis_index("col")
    width = spread.shape[2]
    remote = functools.partial(pltpu.make_async_remote_copy, device_id_type=MESH)
    contract = functools.partial(lax.dot_general, preferred_element_type=jnp.float32)
    barrier = pltpu.get_barrier_semaphore()

    def each(first, last, action):
        def step(k, carry):
            action(k)
            return carry
        lax.fori_loop(first, last, step, 0)

    def row_peer(k):
        return (lax.rem(row + k, 8), col)

    def col_peer(k):
        return (row, lax.rem(col + k, 16))

    def rows_of(j):
        return pl.ds(pl.multiple_of(j * ROWS, ROWS), ROWS)

    def load(j):
        return pltpu.make_async_copy(raw.at[rows_of(j)], held.at[rows_of(j)], load_sem.at[j])

    def move(j, k):
        target = lax.rem(col + k, 16)
        part = held.at[rows_of(j), pl.ds(pl.multiple_of(target * width, 128), width)]
        return remote(part, spread.at[col, rows_of(j)], move_s.at[j, k], move_r.at[j, k], device_id=(row, target))

    each(0, 8, lambda j: load(j).start())
    each(1, 8, lambda k: pl.semaphore_signal(barrier, 1, device_id=row_peer(k), device_id_type=MESH))
    each(1, 16, lambda k: pl.semaphore_signal(barrier, 1, device_id=col_peer(k), device_id_type=MESH))
    pl.semaphore_wait(barrier, 22)

    def send_rows(j):
        load(j).wait()
        each(1, 16, lambda k: move(j, k).start())

    each(0, EARLY, send_rows)
    each(EARLY, 8, lambda j: load(j).wait())
    own = pltpu.make_async_copy(held.at[:, pl.ds(pl.multiple_of(col * width, 128), width)], spread.at[col], own_sem)
    own.start()

    gram_high[...] = jnp.zeros_like(gram_high)
    gram_low[...] = jnp.zeros_like(gram_low)
    rhs_t = (((1,), (1,)), ((), ()))

    def gram_step(s):
        hi, lo = split(held[:, pl.ds(pl.multiple_of(s * 1024, 1024), 1024)])
        gram_high[...] += contract(hi, hi, rhs_t)
        gram_low[...] += contract(hi, lo, rhs_t)

    each(0, raw.shape[1] // 1024, gram_step)
    lane = lax.broadcasted_iota(jnp.int32, (1, CAP), 1)
    label = jnp.broadcast_to(labels[...], (8, CAP))
    lanes = lax.broadcasted_iota(jnp.int32, (8, CAP), 1)
    offsets = jnp.where((lanes == 0) | (label != pltpu.roll(label, 1, 1)), lanes, 0)
    for bit in range(5):
        shift = 1 << bit
        offsets = jnp.maximum(offsets, jnp.where(lanes >= shift, pltpu.roll(offsets, shift, 1), 0))
    offset = offsets[:1]
    own_start, own_count = jnp.int32(0), jnp.int32(0)
    for t in range(16):
        own_start = own_start + jnp.where(t < col, counts[t], 0)
        own_count = own_count + jnp.where(t == col, counts[t], 0)
    live = lane < own_count
    low = gram_low[...]
    window[...] = cluster_window(gram_high[...] + (low + low.T), offset)
    one_hi, one_lo = split(panel_one[...])
    two_hi, two_lo = split(panel_two[...])
    turned_hi, turned_lo = two_hi.T, two_lo.T
    cross[...] = dot3(turned_hi, turned_lo, one_hi, one_lo)
    v_hi[:, :CAP], v_hi[:, CAP:] = two_hi, one_hi
    v_lo[:, :CAP], v_lo[:, CAP:] = two_lo, one_lo

    def window_copy(k):
        return remote(window, window_in.at[k], win_s.at[k], win_r.at[k], device_id=row_peer(k))

    def cross_copy(k):
        return remote(cross.at[rows_of(lax.rem(row + k, 8))], cross_in.at[k], cr_s.at[k], cr_r.at[k], device_id=row_peer(k))

    each(1, 8, lambda k: window_copy(k).start())
    each(1, 8, lambda k: cross_copy(k).start())
    each(1, 8, lambda k: window_copy(k).wait())
    each(1, 8, lambda k: cross_copy(k).wait())
    piece = cross[rows_of(row)]
    for k in range(1, 8):
        piece = piece + cross_in[k]
    cross_mine[...] = piece
    window_in[0] = window[...]
    total = window_in[row]
    for r in range(1, 8):
        total = total + window_in[lax.rem(row + 8 - r, 8)]
    band[:CM] = inverse_band(total, offset, live)
    band[CM:CM + 1] = offset.astype(jnp.float32)
    band[CM + 1:CM + 2] = jnp.broadcast_to(lax.rem(own_start, 8), (1, CAP)).astype(jnp.float32)
    band[CM + 2:] = jnp.zeros((6, CAP), jnp.float32)

    def band_copy(k):
        return remote(band, bands.at[col], bd_s.at[k], bd_r.at[k], device_id=col_peer(k))

    def cross_all_copy(k):
        return remote(cross_mine, cross_all.at[k], ca_s.at[k], ca_r.at[k], device_id=col_peer(k))

    def cross_share_copy(k):
        spot = cross_sum.at[rows_of(row)]
        return remote(spot, spot, cg_s.at[k], cg_r.at[k], device_id=row_peer(k))

    each(1, 16, lambda k: cross_all_copy(k).start())
    each(1, 16, lambda k: band_copy(k).start())
    for j in range(EARLY, 8):
        each(1, 16, lambda k: move(j, k).start())
    bands[col] = band[...]
    f_hi, f_lo = split(factor_one[...].T)
    one = contract(f_hi, one_hi, rhs_t) + (contract(f_hi, one_lo, rhs_t) + contract(f_lo, one_hi, rhs_t))
    hi, lo = split(one)
    b_hi[CAP:], b_lo[CAP:] = hi, lo
    each(1, 16, lambda k: cross_all_copy(k).wait())
    piece = cross_mine[...]
    for k in range(1, 16):
        piece = piece + cross_all[k]
    cross_sum[rows_of(row)] = piece
    each(1, 8, lambda k: cross_share_copy(k).start())
    each(1, 16, lambda k: band_copy(k).wait())

    def widen(s):
        hi, lo = split(dense_rows(bands[s, :CM], bands[s, CM:CM + 1].astype(jnp.int32), bands[s, CM + 1:CM + 2].astype(jnp.int32)))
        t_hi[s], t_lo[s] = hi, lo

    each(0, 16, widen)
    each(1, 8, lambda k: cross_share_copy(k).wait())
    c_hi, c_lo = split(cross_sum[...])
    rest_hi, rest_lo = split(panel_two[...].T - dot3(c_hi, c_lo, b_hi[CAP:], b_lo[CAP:]))
    f_hi, f_lo = split(factor_two[...].T)
    hi, lo = split(dot3(f_hi, f_lo, rest_hi, rest_lo))
    b_hi[:CAP], b_lo[:CAP] = hi, lo
    own.wait()

    def finish(j):
        each(1, 16, lambda k: move(j, k).wait())

    each(0, 8, finish)


def front(counts, raw, labels, panel_one, factor_one, panel_two, factor_two):
    D, V = pltpu.SemaphoreType.DMA, pltpu.VMEM
    width = raw.shape[1] // 16
    vmem = pl.BlockSpec(memory_space=pltpu.VMEM)
    hbm = pl.BlockSpec(memory_space=pl.ANY)
    half = lambda *shape: jax.ShapeDtypeStruct(shape, jnp.bfloat16)
    tile = lambda *shape: V((*shape, CAP), jnp.float32)
    return pl.pallas_call(
        front_kernel,
        out_shape=(
            jax.ShapeDtypeStruct((16, CAP, width), jnp.float32),
            half(16, TALL, CAP), half(16, TALL, CAP), half(width, 512), half(width, 512), half(512, width), half(512, width),
        ),
        in_specs=[pl.BlockSpec(memory_space=pltpu.SMEM), hbm, vmem, vmem, vmem, vmem, vmem],
        out_specs=(hbm, vmem, vmem, vmem, vmem, vmem, vmem),
        scratch_shapes=[
            V(raw.shape, jnp.float32), tile(CAP), tile(CAP), tile(CAP), tile(CM), tile(8, CM), tile(8, ROWS), tile(ROWS),
            tile(16, ROWS), tile(CAP), tile(40), tile(16, 40),
            D((8,)), D, D((8, 16)), D((8, 16)), D((8,)), D((8,)), D((8,)), D((8,)), D((16,)), D((16,)), D((8,)), D((8,)),
            D((16,)), D((16,)),
        ],
        compiler_params=pltpu.CompilerParams(collective_id=3, has_side_effects=True, vmem_limit_bytes=56 * 1024 * 1024),
    )(counts, raw, labels, panel_one, factor_one, panel_two, factor_two)


def order_kernel(start_ref, t_hi, t_lo, raw_ref, held):
    start = start_ref[pl.program_id(0)]
    lead = lax.rem(start, 8)
    base = pl.multiple_of(start - lead, 8)
    z_hi, z_lo = split(raw_ref[0])
    rows = dot3(t_hi[0], t_lo[0], z_hi, z_lo)
    kept = lax.broadcasted_iota(jnp.int32, (8, rows.shape[1]), 0) < lead
    held[pl.ds(base, 8), :] = jnp.where(kept, held[pl.ds(base, 8), :], rows[:8])
    held[pl.ds(base + 8, CAP), :] = rows[8:CAP + 8]


def order_rows(starts, t_hi, t_lo, spread):
    width = spread.shape[2]
    factor = pl.BlockSpec((1, TALL, CAP), lambda s, starts: (s, 0, 0))
    return pl.pallas_call(
        order_kernel,
        grid_spec=pltpu.PrefetchScalarGridSpec(
            num_scalar_prefetch=1,
            grid=(16,),
            in_specs=[factor, factor, pl.BlockSpec((1, CAP, width), lambda s, starts: (s, 0, 0))],
            out_specs=pl.BlockSpec((2048 + CAP + 8, width), lambda s, starts: (0, 0)),
        ),
        out_shape=jax.ShapeDtypeStruct((2048 + CAP + 8, width), jnp.float32),
    )(starts, t_hi, t_lo, spread)


def body(raw_vectors, interval_count, cluster_of, panel_one, factor_one, panel_two, factor_two):
    spread, t_hi, t_lo, v_hi, v_lo, b_hi, b_lo = front(
        interval_count, raw_vectors, cluster_of, panel_one, factor_one, panel_two, factor_two
    )
    starts = jnp.cumsum(interval_count) - interval_count
    ordered = order_rows(starts, t_hi, t_lo, spread)
    return back_transform(ordered, v_hi, v_lo, b_hi, b_lo)


def solution(mesh):
    placed = (
        P("col", "row"),
        P(),
        P("col", None),
        P(("row", "col"), None),
        P(),
        P(("row", "col"), None),
        P(),
    )
    return jax.shard_map(
        body, mesh=mesh, in_specs=placed, out_specs=P("col", "row"), check_vma=False
    )
```

```python
import functools
import math

import jax
import jax.numpy as jnp
from jax import lax
from jax.experimental import pallas as pl
from jax.experimental.pallas import tpu as pltpu
from jax.sharding import PartitionSpec as P

N = 81920
CAP = 256
CM = 32
TALL = 272
MESH = pl.DeviceIdType.MESH


def split(value):
    hi = value.astype(jnp.bfloat16)
    return hi, (value - hi.astype(jnp.float32)).astype(jnp.bfloat16)


def dot3(a_hi, a_lo, b_hi, b_lo):
    mul = functools.partial(jnp.dot, preferred_element_type=jnp.float32)
    return mul(a_hi, b_hi) + (mul(a_hi, b_lo) + mul(a_lo, b_hi))


CHUNKS = 8


def back_transform_kernel(
    rows_in, v_hi_in, v_lo_in, b_hi_in, b_lo_in, out,
    ordered_rows, v_hi, v_lo, b_hi, b_lo, part, core_in, acc, ring_a, ring_b, plane_in, whole, result,
    core_s, core_r, ra_s, ra_r, rb_s, rb_r, ps_s, ps_r, pg_s, pg_r, ga_s, ga_r, gb_s, gb_r, gc_s, gc_r,
    move_s, move_r, own_sem, rows_sem, panel_sem,
):
    row, col = lax.axis_index("row"), lax.axis_index("col")
    core, x = lax.rem(row, 2), lax.div(row, 2)
    width = ordered_rows.shape[1]
    partner = (x * 2 + 1 - core, col)
    right = (lax.rem(x + 1, 4) * 2 + core, col)
    left = (lax.rem(x + 3, 4) * 2 + core, col)
    mine, other = core * 16, (1 - core) * 16
    here = x * 4
    after, before, far = lax.rem(x + 1, 4) * 4, lax.rem(x + 3, 4) * 4, lax.rem(x + 2, 4) * 4

    remote = functools.partial(pltpu.make_async_remote_copy, device_id_type=MESH)

    panels = [
        pltpu.make_async_copy(source, target, panel_sem.at[i])
        for i, (source, target) in enumerate(((v_hi_in, v_hi), (v_lo_in, v_lo), (b_hi_in, b_hi), (b_lo_in, b_lo)))
    ]

    def load(c):
        rows = pl.ds(pl.multiple_of(c * 256, 256), 256)
        return pltpu.make_async_copy(rows_in.at[rows], ordered_rows.at[rows], rows_sem.at[c])

    panels[0].start()
    panels[1].start()
    for c in range(CHUNKS):
        load(c).start()
    panels[2].start()
    panels[3].start()
    barrier = pltpu.get_barrier_semaphore()

    def greet(device):
        pl.semaphore_signal(barrier, 1, device_id=device, device_id_type=MESH)

    for device in (partner, right, left):
        greet(device)

    def greet_column(k, carry):
        greet((row, lax.rem(col + k, 16)))
        return carry

    lax.fori_loop(1, 16, greet_column, 0)
    pl.semaphore_wait(barrier, 18)
    panels[0].wait()
    panels[1].wait()

    def core_copy(c):
        return remote(part.at[c, pl.ds(other, 16)], core_in.at[c], core_s.at[c], core_r.at[c], device_id=partner)

    def ring_a_copies(c):
        return (
            remote(acc.at[c, pl.ds(far, 2)], ring_a.at[c, pl.ds(0, 2)], ra_s.at[c, 0], ra_r.at[c, 0], device_id=right),
            remote(acc.at[c, pl.ds(far + 2, 2)], ring_a.at[c, pl.ds(2, 2)], ra_s.at[c, 1], ra_r.at[c, 1], device_id=left),
        )

    def ring_b_copies(c):
        return (
            remote(acc.at[c, pl.ds(after, 4)], ring_b.at[c, 0], rb_s.at[c, 0], rb_r.at[c, 0], device_id=right),
            remote(acc.at[c, pl.ds(before, 4)], ring_b.at[c, 1], rb_s.at[c, 1], rb_r.at[c, 1], device_id=left),
        )

    def plane_copy(c, k):
        peer = lax.rem(col + k, 16)
        source = acc.at[c, here + lax.div(peer, 4), lax.rem(peer, 4)]
        return remote(source, plane_in.at[c, k], ps_s.at[c, k], ps_r.at[c, k], device_id=(row, peer))

    def gather_copy(c, k):
        spot = whole.at[c, mine + here + lax.div(col, 4), lax.rem(col, 4)]
        return remote(spot, spot, pg_s.at[c, k], pg_r.at[c, k], device_id=(row, lax.rem(col + k, 16)))

    def spread_copies(c):
        spot = whole.at[c, pl.ds(mine + here, 4)]
        return (
            remote(spot, spot, ga_s.at[c, 0], ga_r.at[c, 0], device_id=right),
            remote(spot, spot, ga_s.at[c, 1], ga_r.at[c, 1], device_id=left),
        )

    def forward_copies(c):
        first, second = whole.at[c, pl.ds(mine + before, 2)], whole.at[c, pl.ds(mine + after + 2, 2)]
        return (
            remote(first, first, gb_s.at[c, 0], gb_r.at[c, 0], device_id=right),
            remote(second, second, gb_s.at[c, 1], gb_r.at[c, 1], device_id=left),
        )

    def share_copy(c):
        spot = whole.at[c, pl.ds(mine, 16)]
        return remote(spot, spot, gc_s.at[c], gc_r.at[c], device_id=partner)

    def window(c, source):
        return out.at[pl.ds(pl.multiple_of(c * 16, 16), 16), pl.ds(pl.multiple_of(source * width, 128), width)]

    def slab(c, target):
        return result.at[c, pl.ds(pl.multiple_of(target * 16, 16), 16)]

    def move_copy(c, k):
        target = lax.rem(col + k, 16)
        return remote(slab(c, target), window(c, col), move_s.at[c, k], move_r.at[c, k], device_id=(row, target))

    def own_copy(c):
        return pltpu.make_async_copy(slab(c, col), window(c, col), own_sem.at[c])

    def start(*copies):
        for copy in copies:
            copy.start()

    def wait(*copies):
        for copy in copies:
            copy.wait()

    def each(first, last, action):
        def step(k, carry):
            action(k)
            return carry
        lax.fori_loop(first, last, step, 0)

    def ordered(c):
        return ordered_rows[pl.ds(pl.multiple_of(c * 256, 256), 256), :]

    def project(c):
        load(c).wait()
        r_hi, r_lo = split(ordered(c))
        product = dot3(r_hi, r_lo, v_hi[...], v_lo[...])
        for q in range(4):
            part[c, :, q] = product[:, q * 128:(q + 1) * 128].reshape(32, 8, 128)
        start(core_copy(c))

    def fold_core(c):
        wait(core_copy(c))
        acc[c] = part[c, pl.ds(mine, 16)] + core_in[c]
        start(*ring_a_copies(c))

    def fold_a(c):
        wait(*ring_a_copies(c))
        acc[c, pl.ds(after, 2)] += ring_a[c, 0:2]
        acc[c, pl.ds(before + 2, 2)] += ring_a[c, 2:4]
        start(*ring_b_copies(c))

    def fold_b(c):
        wait(*ring_b_copies(c))
        acc[c, pl.ds(here, 4)] += ring_b[c, 0] + ring_b[c, 1]
        each(1, 16, lambda k: plane_copy(c, k).start())

    def fold_plane(c):
        each(1, 16, lambda k: plane_copy(c, k).wait())
        total = acc[c, here + lax.div(col, 4), lax.rem(col, 4)]
        for k in range(1, 16):
            total = total + plane_in[c, k]
        whole[c, mine + here + lax.div(col, 4), lax.rem(col, 4)] = total
        each(1, 16, lambda k: gather_copy(c, k).start())

    def gather_plane(c):
        each(1, 16, lambda k: gather_copy(c, k).wait())
        start(*spread_copies(c))

    def forward(c):
        wait(*spread_copies(c))
        start(*forward_copies(c))

    def share(c):
        wait(*forward_copies(c))
        start(share_copy(c))

    def correct(c):
        wait(share_copy(c))
        x_hi, x_lo = split(jnp.concatenate([whole[c, :, q].reshape(256, 128) for q in range(4)], axis=1))
        result[c] = ordered(c) - dot3(x_hi, x_lo, b_hi[...], b_lo[...])
        each(1, 16, lambda k: move_copy(c, k).start())
        own_copy(c).start()

    stages = (
        (1, fold_core), (2, fold_a), (3, fold_b), (5, fold_plane), (7, gather_plane), (8, forward), (9, share),
        (10, correct), (0, project),
    )

    def tick(t, carry):
        for lag, stage in stages:
            c = t - lag

            @pl.when((c >= 0) & (c < CHUNKS))
            def _(stage=stage, c=c):
                stage(c)

        return carry

    lax.fori_loop(0, 8, tick, 0)
    panels[2].wait()
    panels[3].wait()
    lax.fori_loop(8, CHUNKS + 10, tick, 0)

    def finish(c):
        each(1, 16, lambda k: move_copy(c, k).wait())
        own_copy(c).wait()

    each(0, CHUNKS, finish)


def back_transform(ordered, v_hi, v_lo, b_hi, b_lo):
    width = v_hi.shape[0]
    D, V = pltpu.SemaphoreType.DMA, pltpu.VMEM
    pair = [D((CHUNKS, 2)), D((CHUNKS, 2))]
    many = [D((CHUNKS, 16)), D((CHUNKS, 16))]
    one = [D((CHUNKS,)), D((CHUNKS,))]
    tile = lambda *lead: V((*lead, 8, 128), jnp.float32)
    return pl.pallas_call(
        back_transform_kernel,
        out_shape=jax.ShapeDtypeStruct((128, 16 * width), jnp.float32),
        in_specs=[pl.BlockSpec(memory_space=pl.ANY)] * 5,
        out_specs=pl.BlockSpec(memory_space=pl.ANY),
        scratch_shapes=[
            V((256 * CHUNKS, width), jnp.float32), V((width, 512), jnp.bfloat16), V((width, 512), jnp.bfloat16),
            V((512, width), jnp.bfloat16), V((512, width), jnp.bfloat16),
            tile(CHUNKS, 32, 4), tile(CHUNKS, 16, 4), tile(CHUNKS, 16, 4), tile(CHUNKS, 4, 4), tile(CHUNKS, 2, 4, 4),
            tile(CHUNKS, 16), tile(CHUNKS, 32, 4), V((CHUNKS, 256, width), jnp.float32),
            *one, *pair, *pair, *many, *many, *pair, *pair, *one, *many, D((CHUNKS,)), D((CHUNKS,)), D((4,)),
        ],
        compiler_params=pltpu.CompilerParams(collective_id=7, has_side_effects=True, vmem_limit_bytes=60 * 1024 * 1024),
    )(ordered, v_hi, v_lo, b_hi, b_lo)


ROWS = CAP // 8


def inverse_band(window, offset, live):
    lane = lax.broadcasted_iota(jnp.int32, (1, CAP), 1)
    position = lane - offset
    sub = lax.broadcasted_iota(jnp.int32, (CM, CAP), 0)
    state = window
    for k in range(CM - 1):
        active = (position > k) & live
        distance = jnp.where(active, position - k, 0)
        pivot_row = state
        for bit in range(5):
            take = jnp.broadcast_to(((distance >> bit) & 1) == 1, (CM, CAP))
            pivot_row = jnp.where(take, pltpu.roll(pivot_row, 1 << bit, 1), pivot_row)
        pivot = jnp.where(active, pivot_row[k:k + 1], 1.0)
        multiplier = jnp.where(active, state[k:k + 1] / pivot, 0.0)
        state = jnp.where(sub == k, jnp.where(active, -multiplier, state), state - multiplier * pivot_row)
    spot = jnp.broadcast_to(position, (CM, CAP))
    diagonal = jnp.sum(jnp.where(sub == spot, state, 0.0), axis=0, keepdims=True)
    scale = math.sqrt(N) / jnp.sqrt(jnp.where(live, diagonal, 1.0))
    rows = jnp.where(sub < spot, state, jnp.where(sub == spot, 1.0, 0.0)) * scale
    return jnp.where(live, rows, 0.0)


def cluster_window(gram, offset):
    window = gram
    for bit, keep in ((7, 160), (6, 96), (5, 64), (4, 48), (3, 40)):
        shift = 1 << bit
        moved = jnp.concatenate([window[shift:], window[:shift]], axis=0)[:keep]
        window = jnp.where(((offset >> bit) & 1) == 1, moved, window[:keep])
    for bit in (2, 1, 0):
        moved = pltpu.roll(window, 40 - (1 << bit), 0)
        window = jnp.where(((offset >> bit) & 1) == 1, moved, window)
    return window[:CM]


def dense_rows(band, offset, lead):
    wide = jnp.concatenate([band, jnp.zeros((8, CAP), jnp.float32)], axis=0)
    for bit in (0, 1, 2):
        wide = jnp.where(((offset >> bit) & 1) == 1, pltpu.roll(wide, 1 << bit, 0), wide)
    for bit, size in ((3, 48), (4, 64), (5, 96), (6, 160), (7, 256)):
        shift = 1 << bit
        have = wide.shape[0]
        plain = jnp.concatenate([wide, jnp.zeros((size - have, CAP), jnp.float32)], axis=0)
        take = min(have, size - shift)
        parts = [jnp.zeros((shift, CAP), jnp.float32), wide[:take]]
        if size - shift - take:
            parts.append(jnp.zeros((size - shift - take, CAP), jnp.float32))
        wide = jnp.where(((offset >> bit) & 1) == 1, jnp.concatenate(parts, axis=0), plain)
    dense = jnp.concatenate([wide.T, jnp.zeros((TALL - CAP, CAP), jnp.float32)], axis=0)
    for bit in range(3):
        dense = jnp.where(((lead >> bit) & 1) == 1, pltpu.roll(dense, 1 << bit, 0), dense)
    return dense


def front_kernel(
    counts, raw, labels, panel_one, factor_one, panel_two, factor_two,
    spread, t_hi, t_lo, v_hi, v_lo, b_hi, b_lo,
    held, gram_high, gram_low, cross, window, window_in, cross_in, cross_mine, cross_y, cross_z, cross_part, cross_sum,
    band, bands, wide_hi, wide_lo,
    load_sem, own_sem, move_s, move_r, win_s, win_r, cr_s, cr_r, cy_s, cy_r, cz_s, cz_r, cp_s, cp_r, cg_s, cg_r,
    bd_s, bd_r, wide_sem,
):
    row, col = lax.axis_index("row"), lax.axis_index("col")
    width = spread.shape[2]
    remote = functools.partial(pltpu.make_async_remote_copy, device_id_type=MESH)
    contract = functools.partial(lax.dot_general, preferred_element_type=jnp.float32)
    barrier = pltpu.get_barrier_semaphore()

    def each(first, last, action):
        def step(k, carry):
            action(k)
            return carry
        lax.fori_loop(first, last, step, 0)

    def row_peer(k):
        return (lax.rem(row + k, 8), col)

    def col_peer(k):
        return (row, lax.rem(col + k, 16))

    def rows_of(j):
        return pl.ds(pl.multiple_of(j * ROWS, ROWS), ROWS)

    def load(j):
        return pltpu.make_async_copy(raw.at[rows_of(j)], held.at[rows_of(j)], load_sem.at[j])

    def move(j, k):
        target = lax.rem(col + k, 16)
        part = held.at[rows_of(j), pl.ds(pl.multiple_of(target * width, 128), width)]
        return remote(part, spread.at[col, rows_of(j)], move_s.at[j, k], move_r.at[j, k], device_id=(row, target))

    each(0, 8, lambda j: load(j).start())
    each(1, 8, lambda k: pl.semaphore_signal(barrier, 1, device_id=row_peer(k), device_id_type=MESH))
    each(1, 16, lambda k: pl.semaphore_signal(barrier, 1, device_id=col_peer(k), device_id_type=MESH))
    pl.semaphore_wait(barrier, 22)

    def send_rows(j):
        load(j).wait()
        each(1, 16, lambda k: move(j, k).start())

    y, z = lax.rem(col, 4), lax.div(col, 4)
    rhs_t = (((1,), (1,)), ((), ()))

    def y_peer(k):
        return (row, z * 4 + lax.rem(y + k, 4))

    def z_peer(k):
        return (row, lax.rem(z + k, 4) * 4 + y)

    def eight(i):
        return pl.ds(pl.multiple_of(i * 8, 8), 8)

    def cross_copy(k):
        return remote(cross.at[rows_of(lax.rem(row + k, 8))], cross_in.at[k], cr_s.at[k], cr_r.at[k], device_id=row_peer(k))

    def cross_y_copy(k):
        return remote(cross_mine.at[eight(lax.rem(y + k, 4))], cross_y.at[k], cy_s.at[k], cy_r.at[k], device_id=y_peer(k))

    def cross_z_copy(k):
        return remote(cross_z.at[0], cross_z.at[k], cz_s.at[k], cz_r.at[k], device_id=z_peer(k))

    def cross_part_copy(k):
        spot = cross_part.at[eight(y)]
        return remote(spot, spot, cp_s.at[k], cp_r.at[k], device_id=y_peer(k))

    def cross_share_copy(k):
        spot = cross_sum.at[rows_of(row)]
        return remote(spot, spot, cg_s.at[k], cg_r.at[k], device_id=row_peer(k))

    def window_copy(k):
        return remote(window, window_in.at[k], win_s.at[k], win_r.at[k], device_id=row_peer(k))

    def band_copy(k):
        return remote(band, bands.at[col], bd_s.at[k], bd_r.at[k], device_id=col_peer(k))

    send_rows(0)
    one_hi, one_lo = split(panel_one[...])
    two_hi, two_lo = split(panel_two[...])
    cross[...] = dot3(two_hi.T, two_lo.T, one_hi, one_lo)
    v_hi[:, :CAP], v_hi[:, CAP:] = two_hi, one_hi
    v_lo[:, :CAP], v_lo[:, CAP:] = two_lo, one_lo
    each(1, 8, lambda k: cross_copy(k).start())
    gram_high[...] = jnp.zeros_like(gram_high)
    gram_low[...] = jnp.zeros_like(gram_low)
    each(1, 8, lambda k: cross_copy(k).wait())
    piece = cross[rows_of(row)]
    for k in range(1, 8):
        piece = piece + cross_in[k]
    cross_mine[...] = piece
    each(1, 4, lambda k: cross_y_copy(k).start())
    each(1, 3, send_rows)
    each(3, 8, lambda j: load(j).wait())
    own = pltpu.make_async_copy(held.at[:, pl.ds(pl.multiple_of(col * width, 128), width)], spread.at[col], own_sem)
    own.start()

    def gram_step(s):
        hi, lo = split(held[:, pl.ds(pl.multiple_of(s * 1024, 1024), 1024)])
        gram_high[...] += contract(hi, hi, rhs_t)
        gram_low[...] += contract(hi, lo, rhs_t)

    each(0, raw.shape[1] // 1024, gram_step)
    lane = lax.broadcasted_iota(jnp.int32, (1, CAP), 1)
    label = jnp.broadcast_to(labels[...], (8, CAP))
    lanes = lax.broadcasted_iota(jnp.int32, (8, CAP), 1)
    offsets = jnp.where((lanes == 0) | (label != pltpu.roll(label, 1, 1)), lanes, 0)
    for bit in range(5):
        shift = 1 << bit
        offsets = jnp.maximum(offsets, jnp.where(lanes >= shift, pltpu.roll(offsets, shift, 1), 0))
    offset = offsets[:1]
    own_count = jnp.int32(0)
    for t in range(16):
        own_count = own_count + jnp.where(t == col, counts[t], 0)
    live = lane < own_count
    low = gram_low[...]
    window[...] = cluster_window(gram_high[...] + (low + low.T), offset)
    each(1, 8, lambda k: window_copy(k).start())
    each(1, 4, lambda k: cross_y_copy(k).wait())
    piece = cross_mine[eight(y)]
    for k in range(1, 4):
        piece = piece + cross_y[k]
    cross_z[0] = piece
    each(1, 4, lambda k: cross_z_copy(k).start())
    each(3, 4, lambda j: each(1, 16, lambda k: move(j, k).start()))
    each(1, 8, lambda k: window_copy(k).wait())
    window_in[0] = window[...]
    total = window_in[row]
    for r in range(1, 8):
        total = total + window_in[lax.rem(row + 8 - r, 8)]
    band[...] = inverse_band(total, offset, live)
    each(1, 16, lambda k: band_copy(k).start())
    bands[col] = band[...]
    each(1, 4, lambda k: cross_z_copy(k).wait())
    piece = cross_z[0]
    for k in range(1, 4):
        piece = piece + cross_z[k]
    cross_part[eight(y)] = piece
    each(1, 4, lambda k: cross_part_copy(k).start())
    each(4, 8, lambda j: each(1, 16, lambda k: move(j, k).start()))
    f_hi, f_lo = split(factor_one[...].T)
    one = contract(f_hi, one_hi, rhs_t) + (contract(f_hi, one_lo, rhs_t) + contract(f_lo, one_hi, rhs_t))
    hi, lo = split(one)
    b_hi[CAP:], b_lo[CAP:] = hi, lo
    each(1, 4, lambda k: cross_part_copy(k).wait())
    cross_sum[rows_of(row)] = cross_part[...]
    each(1, 8, lambda k: cross_share_copy(k).start())
    each(1, 16, lambda k: band_copy(k).wait())
    depth = lax.broadcasted_iota(jnp.int32, (CM, CAP), 0)

    def wide_copies(s):
        return (
            pltpu.make_async_copy(wide_hi.at[s], t_hi.at[s], wide_sem.at[s, 0]),
            pltpu.make_async_copy(wide_lo.at[s], t_lo.at[s], wide_sem.at[s, 1]),
        )

    def widen(s):
        start = jnp.int32(0)
        for t in range(16):
            start = start + jnp.where(t < s, counts[t], 0)
        rows = bands[s]
        last = jnp.max(jnp.where(rows != 0.0, depth, 0), axis=0, keepdims=True)
        hi, lo = split(dense_rows(rows, lane - last, jnp.broadcast_to(lax.rem(start, 8), (1, CAP))))
        wide_hi[s], wide_lo[s] = hi, lo
        for copy in wide_copies(s):
            copy.start()

    each(0, 16, widen)
    each(1, 8, lambda k: cross_share_copy(k).wait())
    c_hi, c_lo = split(cross_sum[...])
    rest_hi, rest_lo = split(panel_two[...].T - dot3(c_hi, c_lo, b_hi[CAP:], b_lo[CAP:]))
    f_hi, f_lo = split(factor_two[...].T)
    hi, lo = split(dot3(f_hi, f_lo, rest_hi, rest_lo))
    b_hi[:CAP], b_lo[:CAP] = hi, lo
    own.wait()

    def finish_wide(s):
        for copy in wide_copies(s):
            copy.wait()

    each(0, 16, finish_wide)

    def finish(j):
        each(1, 16, lambda k: move(j, k).wait())

    each(0, 8, finish)


def front(counts, raw, labels, panel_one, factor_one, panel_two, factor_two):
    D, V = pltpu.SemaphoreType.DMA, pltpu.VMEM
    width = raw.shape[1] // 16
    vmem = pl.BlockSpec(memory_space=pltpu.VMEM)
    hbm = pl.BlockSpec(memory_space=pl.ANY)
    half = lambda *shape: jax.ShapeDtypeStruct(shape, jnp.bfloat16)
    tile = lambda *shape: V((*shape, CAP), jnp.float32)
    return pl.pallas_call(
        front_kernel,
        out_shape=(
            jax.ShapeDtypeStruct((16, CAP, width), jnp.float32),
            half(16, TALL, CAP), half(16, TALL, CAP), half(width, 512), half(width, 512), half(512, width), half(512, width),
        ),
        in_specs=[pl.BlockSpec(memory_space=pltpu.SMEM), hbm, vmem, vmem, vmem, vmem, vmem],
        out_specs=(hbm, hbm, hbm, vmem, vmem, vmem, vmem),
        scratch_shapes=[
            V(raw.shape, jnp.float32), tile(CAP), tile(CAP), tile(CAP), tile(CM), tile(8, CM), tile(8, ROWS), tile(ROWS),
            tile(4, 8), tile(4, 8), tile(ROWS), tile(CAP), tile(CM), tile(16, CM),
            V((16, TALL, CAP), jnp.bfloat16), V((16, TALL, CAP), jnp.bfloat16),
            D((8,)), D, D((8, 16)), D((8, 16)), D((8,)), D((8,)), D((8,)), D((8,)), D((4,)), D((4,)), D((4,)), D((4,)),
            D((4,)), D((4,)), D((8,)), D((8,)), D((16,)), D((16,)), D((16, 2)),
        ],
        compiler_params=pltpu.CompilerParams(collective_id=3, has_side_effects=True, vmem_limit_bytes=56 * 1024 * 1024),
    )(counts, raw, labels, panel_one, factor_one, panel_two, factor_two)


def order_kernel(start_ref, t_hi, t_lo, raw_ref, held):
    for i in range(raw_ref.shape[0]):
        start = start_ref[pl.program_id(0) * raw_ref.shape[0] + i]
        lead = lax.rem(start, 8)
        base = pl.multiple_of(start - lead, 8)
        z_hi, z_lo = split(raw_ref[i])
        rows = dot3(t_hi[i], t_lo[i], z_hi, z_lo)
        kept = lax.broadcasted_iota(jnp.int32, (8, rows.shape[1]), 0) < lead
        held[pl.ds(base, 8), :] = jnp.where(kept, held[pl.ds(base, 8), :], rows[:8])
        held[pl.ds(base + 8, CAP), :] = rows[8:CAP + 8]


def order_rows(starts, t_hi, t_lo, spread):
    width = spread.shape[2]
    group = 2
    factor = pl.BlockSpec((group, TALL, CAP), lambda s, starts: (s, 0, 0))
    return pl.pallas_call(
        order_kernel,
        grid_spec=pltpu.PrefetchScalarGridSpec(
            num_scalar_prefetch=1,
            grid=(16 // group,),
            in_specs=[factor, factor, pl.BlockSpec((group, CAP, width), lambda s, starts: (s, 0, 0))],
            out_specs=pl.BlockSpec((2048 + CAP + 8, width), lambda s, starts: (0, 0)),
        ),
        out_shape=jax.ShapeDtypeStruct((2048 + CAP + 8, width), jnp.float32),
    )(starts, t_hi, t_lo, spread)


def body(raw_vectors, interval_count, cluster_of, panel_one, factor_one, panel_two, factor_two):
    spread, t_hi, t_lo, v_hi, v_lo, b_hi, b_lo = front(
        interval_count, raw_vectors, cluster_of, panel_one, factor_one, panel_two, factor_two
    )
    starts = jnp.cumsum(interval_count) - interval_count
    ordered = order_rows(starts, t_hi, t_lo, spread)
    return back_transform(ordered, v_hi, v_lo, b_hi, b_lo)


def solution(mesh):
    placed = (
        P("col", "row"),
        P(),
        P("col", None),
        P(("row", "col"), None),
        P(),
        P(("row", "col"), None),
        P(),
    )
    return jax.shard_map(
        body, mesh=mesh, in_specs=placed, out_specs=P("col", "row"), check_vma=False
    )
```

```python
import functools
import math

import jax
import jax.numpy as jnp
from jax import lax
from jax.experimental import pallas as pl
from jax.experimental.pallas import tpu as pltpu
from jax.sharding import PartitionSpec as P

N = 81920
CAP = 256
CM = 32
TALL = 272
MESH = pl.DeviceIdType.MESH


def split(value):
    hi = value.astype(jnp.bfloat16)
    return hi, (value - hi.astype(jnp.float32)).astype(jnp.bfloat16)


def dot3(a_hi, a_lo, b_hi, b_lo):
    mul = functools.partial(jnp.dot, preferred_element_type=jnp.float32)
    return mul(a_hi, b_hi) + (mul(a_hi, b_lo) + mul(a_lo, b_hi))


CHUNKS = 8


def back_transform_kernel(
    rows_in, v_hi_in, v_lo_in, b_hi_in, b_lo_in, out,
    ordered_rows, v_hi, v_lo, b_hi, b_lo, part, core_in, acc, ring_a, ring_b, plane_in, whole, result,
    core_s, core_r, ra_s, ra_r, rb_s, rb_r, ps_s, ps_r, pg_s, pg_r, ga_s, ga_r, gb_s, gb_r, gc_s, gc_r,
    move_s, move_r, own_sem, rows_sem, panel_sem,
):
    row, col = lax.axis_index("row"), lax.axis_index("col")
    core, x = lax.rem(row, 2), lax.div(row, 2)
    width = ordered_rows.shape[1]
    partner = (x * 2 + 1 - core, col)
    right = (lax.rem(x + 1, 4) * 2 + core, col)
    left = (lax.rem(x + 3, 4) * 2 + core, col)
    mine, other = core * 16, (1 - core) * 16
    here = x * 4
    after, before, far = lax.rem(x + 1, 4) * 4, lax.rem(x + 3, 4) * 4, lax.rem(x + 2, 4) * 4

    remote = functools.partial(pltpu.make_async_remote_copy, device_id_type=MESH)

    panels = [
        pltpu.make_async_copy(source, target, panel_sem.at[i])
        for i, (source, target) in enumerate(((v_hi_in, v_hi), (v_lo_in, v_lo), (b_hi_in, b_hi), (b_lo_in, b_lo)))
    ]

    def load(c):
        rows = pl.ds(pl.multiple_of(c * 256, 256), 256)
        return pltpu.make_async_copy(rows_in.at[rows], ordered_rows.at[rows], rows_sem.at[c])

    panels[0].start()
    panels[1].start()
    for c in range(CHUNKS):
        load(c).start()
    panels[2].start()
    panels[3].start()
    barrier = pltpu.get_barrier_semaphore()

    def greet(device):
        pl.semaphore_signal(barrier, 1, device_id=device, device_id_type=MESH)

    for device in (partner, right, left):
        greet(device)

    def greet_column(k, carry):
        greet((row, lax.rem(col + k, 16)))
        return carry

    lax.fori_loop(1, 16, greet_column, 0)
    pl.semaphore_wait(barrier, 18)
    panels[0].wait()
    panels[1].wait()

    def core_copy(c):
        return remote(part.at[c, pl.ds(other, 16)], core_in.at[c], core_s.at[c], core_r.at[c], device_id=partner)

    def ring_a_copies(c):
        return (
            remote(acc.at[c, pl.ds(far, 2)], ring_a.at[c, pl.ds(0, 2)], ra_s.at[c, 0], ra_r.at[c, 0], device_id=right),
            remote(acc.at[c, pl.ds(far + 2, 2)], ring_a.at[c, pl.ds(2, 2)], ra_s.at[c, 1], ra_r.at[c, 1], device_id=left),
        )

    def ring_b_copies(c):
        return (
            remote(acc.at[c, pl.ds(after, 4)], ring_b.at[c, 0], rb_s.at[c, 0], rb_r.at[c, 0], device_id=right),
            remote(acc.at[c, pl.ds(before, 4)], ring_b.at[c, 1], rb_s.at[c, 1], rb_r.at[c, 1], device_id=left),
        )

    def plane_copy(c, k):
        peer = lax.rem(col + k, 16)
        source = acc.at[c, here + lax.div(peer, 4), lax.rem(peer, 4)]
        return remote(source, plane_in.at[c, k], ps_s.at[c, k], ps_r.at[c, k], device_id=(row, peer))

    def gather_copy(c, k):
        spot = whole.at[c, mine + here + lax.div(col, 4), lax.rem(col, 4)]
        return remote(spot, spot, pg_s.at[c, k], pg_r.at[c, k], device_id=(row, lax.rem(col + k, 16)))

    def spread_copies(c):
        spot = whole.at[c, pl.ds(mine + here, 4)]
        return (
            remote(spot, spot, ga_s.at[c, 0], ga_r.at[c, 0], device_id=right),
            remote(spot, spot, ga_s.at[c, 1], ga_r.at[c, 1], device_id=left),
        )

    def forward_copies(c):
        first, second = whole.at[c, pl.ds(mine + before, 2)], whole.at[c, pl.ds(mine + after + 2, 2)]
        return (
            remote(first, first, gb_s.at[c, 0], gb_r.at[c, 0], device_id=right),
            remote(second, second, gb_s.at[c, 1], gb_r.at[c, 1], device_id=left),
        )

    def share_copy(c):
        spot = whole.at[c, pl.ds(mine, 16)]
        return remote(spot, spot, gc_s.at[c], gc_r.at[c], device_id=partner)

    def window(c, source):
        return out.at[source, pl.ds(pl.multiple_of(c * 16, 16), 16)]

    def slab(c, target):
        return result.at[c, pl.ds(pl.multiple_of(target * 16, 16), 16)]

    def move_copy(c, k):
        target = lax.rem(col + k, 16)
        return remote(slab(c, target), window(c, col), move_s.at[c, k], move_r.at[c, k], device_id=(row, target))

    def own_copy(c):
        return pltpu.make_async_copy(slab(c, col), window(c, col), own_sem.at[c])

    def start(*copies):
        for copy in copies:
            copy.start()

    def wait(*copies):
        for copy in copies:
            copy.wait()

    def each(first, last, action):
        def step(k, carry):
            action(k)
            return carry
        lax.fori_loop(first, last, step, 0)

    def ordered(c):
        return ordered_rows[pl.ds(pl.multiple_of(c * 256, 256), 256), :]

    def project(c):
        load(c).wait()
        r_hi, r_lo = split(ordered(c))
        product = dot3(r_hi, r_lo, v_hi[...], v_lo[...])
        for q in range(4):
            part[c, :, q] = product[:, q * 128:(q + 1) * 128].reshape(32, 8, 128)
        start(core_copy(c))

    def fold_core(c):
        wait(core_copy(c))
        acc[c] = part[c, pl.ds(mine, 16)] + core_in[c]
        start(*ring_a_copies(c))

    def fold_a(c):
        wait(*ring_a_copies(c))
        acc[c, pl.ds(after, 2)] += ring_a[c, 0:2]
        acc[c, pl.ds(before + 2, 2)] += ring_a[c, 2:4]
        start(*ring_b_copies(c))

    def fold_b(c):
        wait(*ring_b_copies(c))
        acc[c, pl.ds(here, 4)] += ring_b[c, 0] + ring_b[c, 1]
        each(1, 16, lambda k: plane_copy(c, k).start())

    def fold_plane(c):
        each(1, 16, lambda k: plane_copy(c, k).wait())
        total = acc[c, here + lax.div(col, 4), lax.rem(col, 4)]
        for k in range(1, 16):
            total = total + plane_in[c, k]
        whole[c, mine + here + lax.div(col, 4), lax.rem(col, 4)] = total
        each(1, 16, lambda k: gather_copy(c, k).start())

    def gather_plane(c):
        each(1, 16, lambda k: gather_copy(c, k).wait())
        start(*spread_copies(c))

    def forward(c):
        wait(*spread_copies(c))
        start(*forward_copies(c))

    def share(c):
        wait(*forward_copies(c))
        start(share_copy(c))

    def correct(c):
        wait(share_copy(c))
        x_hi, x_lo = split(jnp.concatenate([whole[c, :, q].reshape(256, 128) for q in range(4)], axis=1))
        result[c] = ordered(c) - dot3(x_hi, x_lo, b_hi[...], b_lo[...])
        each(1, 16, lambda k: move_copy(c, k).start())
        own_copy(c).start()

    stages = (
        (8, correct), (7, share), (6, forward), (5, gather_plane), (4, fold_plane), (3, fold_b), (2, fold_a),
        (1, fold_core), (0, project),
    )

    def tick(t, carry):
        for lag, stage in stages:
            c = t - lag

            @pl.when((c >= 0) & (c < CHUNKS))
            def _(stage=stage, c=c):
                stage(c)

        return carry

    lax.fori_loop(0, 8, tick, 0)
    panels[2].wait()
    panels[3].wait()
    lax.fori_loop(8, CHUNKS + 8, tick, 0)

    def finish(c):
        each(1, 16, lambda k: move_copy(c, k).wait())
        own_copy(c).wait()

    each(0, CHUNKS, finish)


def back_transform(ordered, v_hi, v_lo, b_hi, b_lo):
    width = v_hi.shape[0]
    D, V = pltpu.SemaphoreType.DMA, pltpu.VMEM
    pair = [D((CHUNKS, 2)), D((CHUNKS, 2))]
    many = [D((CHUNKS, 16)), D((CHUNKS, 16))]
    one = [D((CHUNKS,)), D((CHUNKS,))]
    tile = lambda *lead: V((*lead, 8, 128), jnp.float32)
    return pl.pallas_call(
        back_transform_kernel,
        out_shape=jax.ShapeDtypeStruct((16, 16 * CHUNKS, width), jnp.float32),
        in_specs=[pl.BlockSpec(memory_space=pl.ANY)] * 5,
        out_specs=pl.BlockSpec(memory_space=pl.ANY),
        scratch_shapes=[
            V((256 * CHUNKS, width), jnp.float32), V((width, 512), jnp.bfloat16), V((width, 512), jnp.bfloat16),
            V((512, width), jnp.bfloat16), V((512, width), jnp.bfloat16),
            tile(CHUNKS, 32, 4), tile(CHUNKS, 16, 4), tile(CHUNKS, 16, 4), tile(CHUNKS, 4, 4), tile(CHUNKS, 2, 4, 4),
            tile(CHUNKS, 16), tile(CHUNKS, 32, 4), V((CHUNKS, 256, width), jnp.float32),
            *one, *pair, *pair, *many, *many, *pair, *pair, *one, *many, D((CHUNKS,)), D((CHUNKS,)), D((4,)),
        ],
        compiler_params=pltpu.CompilerParams(collective_id=7, has_side_effects=True, vmem_limit_bytes=60 * 1024 * 1024),
    )(ordered, v_hi, v_lo, b_hi, b_lo)


ROWS = CAP // 8


def inverse_band(window, offset, live):
    lane = lax.broadcasted_iota(jnp.int32, (1, CAP), 1)
    position = lane - offset
    sub = lax.broadcasted_iota(jnp.int32, (CM, CAP), 0)
    state = window
    for k in range(CM - 1):
        active = (position > k) & live
        distance = jnp.where(active, position - k, 0)
        pivot_row = state
        for bit in range(5):
            take = jnp.broadcast_to(((distance >> bit) & 1) == 1, (CM, CAP))
            pivot_row = jnp.where(take, pltpu.roll(pivot_row, 1 << bit, 1), pivot_row)
        pivot = jnp.where(active, pivot_row[k:k + 1], 1.0)
        multiplier = jnp.where(active, state[k:k + 1] / pivot, 0.0)
        state = jnp.where(sub == k, jnp.where(active, -multiplier, state), state - multiplier * pivot_row)
    spot = jnp.broadcast_to(position, (CM, CAP))
    diagonal = jnp.sum(jnp.where(sub == spot, state, 0.0), axis=0, keepdims=True)
    scale = math.sqrt(N) / jnp.sqrt(jnp.where(live, diagonal, 1.0))
    rows = jnp.where(sub < spot, state, jnp.where(sub == spot, 1.0, 0.0)) * scale
    return jnp.where(live, rows, 0.0)


def cluster_window(gram, offset):
    window = gram
    for bit, keep in ((7, 160), (6, 96), (5, 64), (4, 48), (3, 40)):
        shift = 1 << bit
        moved = jnp.concatenate([window[shift:], window[:shift]], axis=0)[:keep]
        window = jnp.where(((offset >> bit) & 1) == 1, moved, window[:keep])
    for bit in (2, 1, 0):
        moved = pltpu.roll(window, 40 - (1 << bit), 0)
        window = jnp.where(((offset >> bit) & 1) == 1, moved, window)
    return window[:CM]


def dense_rows(band, offset, lead):
    wide = jnp.concatenate([band, jnp.zeros((8, CAP), jnp.float32)], axis=0)
    for bit in (0, 1, 2):
        wide = jnp.where(((offset >> bit) & 1) == 1, pltpu.roll(wide, 1 << bit, 0), wide)
    for bit, size in ((3, 48), (4, 64), (5, 96), (6, 160), (7, 256)):
        shift = 1 << bit
        have = wide.shape[0]
        plain = jnp.concatenate([wide, jnp.zeros((size - have, CAP), jnp.float32)], axis=0)
        take = min(have, size - shift)
        parts = [jnp.zeros((shift, CAP), jnp.float32), wide[:take]]
        if size - shift - take:
            parts.append(jnp.zeros((size - shift - take, CAP), jnp.float32))
        wide = jnp.where(((offset >> bit) & 1) == 1, jnp.concatenate(parts, axis=0), plain)
    dense = jnp.concatenate([wide.T, jnp.zeros((TALL - CAP, CAP), jnp.float32)], axis=0)
    for bit in range(3):
        dense = jnp.where(((lead >> bit) & 1) == 1, pltpu.roll(dense, 1 << bit, 0), dense)
    return dense


def front_kernel(
    counts, raw, labels, panel_one, factor_one, panel_two, factor_two,
    spread, t_hi, t_lo, v_hi, v_lo, b_hi, b_lo,
    held, gram_high, gram_low, cross, window, window_in, cross_in, cross_mine, cross_y, cross_z, cross_part, cross_sum,
    band, bands, wide_hi, wide_lo,
    load_sem, own_sem, move_s, move_r, win_s, win_r, cr_s, cr_r, cy_s, cy_r, cz_s, cz_r, cp_s, cp_r, cg_s, cg_r,
    bd_s, bd_r, wide_sem,
):
    row, col = lax.axis_index("row"), lax.axis_index("col")
    width = spread.shape[2]
    remote = functools.partial(pltpu.make_async_remote_copy, device_id_type=MESH)
    contract = functools.partial(lax.dot_general, preferred_element_type=jnp.float32)
    barrier = pltpu.get_barrier_semaphore()

    def each(first, last, action):
        def step(k, carry):
            action(k)
            return carry
        lax.fori_loop(first, last, step, 0)

    def row_peer(k):
        return (lax.rem(row + k, 8), col)

    def col_peer(k):
        return (row, lax.rem(col + k, 16))

    def rows_of(j):
        return pl.ds(pl.multiple_of(j * ROWS, ROWS), ROWS)

    def load(j):
        return pltpu.make_async_copy(raw.at[rows_of(j)], held.at[rows_of(j)], load_sem.at[j])

    def move(j, k):
        target = lax.rem(col + k, 16)
        part = held.at[rows_of(j), pl.ds(pl.multiple_of(target * width, 128), width)]
        return remote(part, spread.at[col, rows_of(j)], move_s.at[j, k], move_r.at[j, k], device_id=(row, target))

    each(0, 8, lambda j: load(j).start())
    each(1, 8, lambda k: pl.semaphore_signal(barrier, 1, device_id=row_peer(k), device_id_type=MESH))
    each(1, 16, lambda k: pl.semaphore_signal(barrier, 1, device_id=col_peer(k), device_id_type=MESH))
    pl.semaphore_wait(barrier, 22)

    def send_rows(j):
        load(j).wait()
        each(1, 16, lambda k: move(j, k).start())

    y, z = lax.rem(col, 4), lax.div(col, 4)
    rhs_t = (((1,), (1,)), ((), ()))

    def y_peer(k):
        return (row, z * 4 + lax.rem(y + k, 4))

    def z_peer(k):
        return (row, lax.rem(z + k, 4) * 4 + y)

    def eight(i):
        return pl.ds(pl.multiple_of(i * 8, 8), 8)

    def cross_copy(k):
        return remote(cross.at[rows_of(lax.rem(row + k, 8))], cross_in.at[k], cr_s.at[k], cr_r.at[k], device_id=row_peer(k))

    def cross_y_copy(k):
        return remote(cross_mine.at[eight(lax.rem(y + k, 4))], cross_y.at[k], cy_s.at[k], cy_r.at[k], device_id=y_peer(k))

    def cross_z_copy(k):
        return remote(cross_z.at[0], cross_z.at[k], cz_s.at[k], cz_r.at[k], device_id=z_peer(k))

    def cross_part_copy(k):
        spot = cross_part.at[eight(y)]
        return remote(spot, spot, cp_s.at[k], cp_r.at[k], device_id=y_peer(k))

    def cross_share_copy(k):
        spot = cross_sum.at[rows_of(row)]
        return remote(spot, spot, cg_s.at[k], cg_r.at[k], device_id=row_peer(k))

    def window_copy(k):
        return remote(window, window_in.at[k], win_s.at[k], win_r.at[k], device_id=row_peer(k))

    def band_copy(k):
        return remote(band, bands.at[col], bd_s.at[k], bd_r.at[k], device_id=col_peer(k))

    send_rows(0)
    one_hi, one_lo = split(panel_one[...])
    two_hi, two_lo = split(panel_two[...])
    cross[...] = dot3(two_hi.T, two_lo.T, one_hi, one_lo)
    v_hi[:, :CAP], v_hi[:, CAP:] = two_hi, one_hi
    v_lo[:, :CAP], v_lo[:, CAP:] = two_lo, one_lo
    each(1, 8, lambda k: cross_copy(k).start())
    gram_high[...] = jnp.zeros_like(gram_high)
    gram_low[...] = jnp.zeros_like(gram_low)
    each(1, 8, lambda k: cross_copy(k).wait())
    piece = cross[rows_of(row)]
    for k in range(1, 8):
        piece = piece + cross_in[k]
    cross_mine[...] = piece
    each(1, 4, lambda k: cross_y_copy(k).start())
    each(1, 3, send_rows)
    each(3, 8, lambda j: load(j).wait())
    own = pltpu.make_async_copy(held.at[:, pl.ds(pl.multiple_of(col * width, 128), width)], spread.at[col], own_sem)
    own.start()

    def gram_step(s):
        hi, lo = split(held[:, pl.ds(pl.multiple_of(s * 1024, 1024), 1024)])
        gram_high[...] += contract(hi, hi, rhs_t)
        gram_low[...] += contract(hi, lo, rhs_t)

    each(0, raw.shape[1] // 1024, gram_step)
    lane = lax.broadcasted_iota(jnp.int32, (1, CAP), 1)
    label = jnp.broadcast_to(labels[...], (8, CAP))
    lanes = lax.broadcasted_iota(jnp.int32, (8, CAP), 1)
    offsets = jnp.where((lanes == 0) | (label != pltpu.roll(label, 1, 1)), lanes, 0)
    for bit in range(5):
        shift = 1 << bit
        offsets = jnp.maximum(offsets, jnp.where(lanes >= shift, pltpu.roll(offsets, shift, 1), 0))
    offset = offsets[:1]
    own_count = jnp.int32(0)
    for t in range(16):
        own_count = own_count + jnp.where(t == col, counts[t], 0)
    live = lane < own_count
    low = gram_low[...]
    window[...] = cluster_window(gram_high[...] + (low + low.T), offset)
    each(1, 8, lambda k: window_copy(k).start())
    each(1, 4, lambda k: cross_y_copy(k).wait())
    piece = cross_mine[eight(y)]
    for k in range(1, 4):
        piece = piece + cross_y[k]
    cross_z[0] = piece
    each(1, 4, lambda k: cross_z_copy(k).start())
    each(3, 4, lambda j: each(1, 16, lambda k: move(j, k).start()))
    each(1, 8, lambda k: window_copy(k).wait())
    window_in[0] = window[...]
    total = window_in[row]
    for r in range(1, 8):
        total = total + window_in[lax.rem(row + 8 - r, 8)]
    band[...] = inverse_band(total, offset, live)
    each(1, 16, lambda k: band_copy(k).start())
    bands[col] = band[...]
    each(1, 4, lambda k: cross_z_copy(k).wait())
    piece = cross_z[0]
    for k in range(1, 4):
        piece = piece + cross_z[k]
    cross_part[eight(y)] = piece
    each(1, 4, lambda k: cross_part_copy(k).start())
    each(4, 8, lambda j: each(1, 16, lambda k: move(j, k).start()))
    f_hi, f_lo = split(factor_one[...].T)
    one = contract(f_hi, one_hi, rhs_t) + (contract(f_hi, one_lo, rhs_t) + contract(f_lo, one_hi, rhs_t))
    hi, lo = split(one)
    b_hi[CAP:], b_lo[CAP:] = hi, lo
    each(1, 4, lambda k: cross_part_copy(k).wait())
    cross_sum[rows_of(row)] = cross_part[...]
    each(1, 8, lambda k: cross_share_copy(k).start())
    each(1, 16, lambda k: band_copy(k).wait())
    depth = lax.broadcasted_iota(jnp.int32, (CM, CAP), 0)

    def wide_copies(s):
        return (
            pltpu.make_async_copy(wide_hi.at[s], t_hi.at[s], wide_sem.at[s, 0]),
            pltpu.make_async_copy(wide_lo.at[s], t_lo.at[s], wide_sem.at[s, 1]),
        )

    def widen(s):
        start = jnp.int32(0)
        for t in range(16):
            start = start + jnp.where(t < s, counts[t], 0)
        rows = bands[s]
        last = jnp.max(jnp.where(rows != 0.0, depth, 0), axis=0, keepdims=True)
        hi, lo = split(dense_rows(rows, lane - last, jnp.broadcast_to(lax.rem(start, 8), (1, CAP))))
        wide_hi[s], wide_lo[s] = hi, lo
        for copy in wide_copies(s):
            copy.start()

    each(0, 16, widen)
    each(1, 8, lambda k: cross_share_copy(k).wait())
    c_hi, c_lo = split(cross_sum[...])
    rest_hi, rest_lo = split(panel_two[...].T - dot3(c_hi, c_lo, b_hi[CAP:], b_lo[CAP:]))
    f_hi, f_lo = split(factor_two[...].T)
    hi, lo = split(dot3(f_hi, f_lo, rest_hi, rest_lo))
    b_hi[:CAP], b_lo[:CAP] = hi, lo
    own.wait()

    def finish_wide(s):
        for copy in wide_copies(s):
            copy.wait()

    each(0, 16, finish_wide)

    def finish(j):
        each(1, 16, lambda k: move(j, k).wait())

    each(0, 8, finish)


def front(counts, raw, labels, panel_one, factor_one, panel_two, factor_two):
    D, V = pltpu.SemaphoreType.DMA, pltpu.VMEM
    width = raw.shape[1] // 16
    vmem = pl.BlockSpec(memory_space=pltpu.VMEM)
    hbm = pl.BlockSpec(memory_space=pl.ANY)
    half = lambda *shape: jax.ShapeDtypeStruct(shape, jnp.bfloat16)
    tile = lambda *shape: V((*shape, CAP), jnp.float32)
    return pl.pallas_call(
        front_kernel,
        out_shape=(
            jax.ShapeDtypeStruct((16, CAP, width), jnp.float32),
            half(16, TALL, CAP), half(16, TALL, CAP), half(width, 512), half(width, 512), half(512, width), half(512, width),
        ),
        in_specs=[pl.BlockSpec(memory_space=pltpu.SMEM), hbm, vmem, vmem, vmem, vmem, vmem],
        out_specs=(hbm, hbm, hbm, vmem, vmem, vmem, vmem),
        scratch_shapes=[
            V(raw.shape, jnp.float32), tile(CAP), tile(CAP), tile(CAP), tile(CM), tile(8, CM), tile(8, ROWS), tile(ROWS),
            tile(4, 8), tile(4, 8), tile(ROWS), tile(CAP), tile(CM), tile(16, CM),
            V((16, TALL, CAP), jnp.bfloat16), V((16, TALL, CAP), jnp.bfloat16),
            D((8,)), D, D((8, 16)), D((8, 16)), D((8,)), D((8,)), D((8,)), D((8,)), D((4,)), D((4,)), D((4,)), D((4,)),
            D((4,)), D((4,)), D((8,)), D((8,)), D((16,)), D((16,)), D((16, 2)),
        ],
        compiler_params=pltpu.CompilerParams(collective_id=3, has_side_effects=True, vmem_limit_bytes=56 * 1024 * 1024),
    )(counts, raw, labels, panel_one, factor_one, panel_two, factor_two)


def order_kernel(counts, t_hi, t_lo, raw_ref, held):
    for i in range(raw_ref.shape[0]):
        start = jnp.int32(0)
        for t in range(16):
            start = start + jnp.where(t < pl.program_id(0) * raw_ref.shape[0] + i, counts[t], 0)
        lead = lax.rem(start, 8)
        base = pl.multiple_of(start - lead, 8)
        z_hi, z_lo = split(raw_ref[i])
        rows = dot3(t_hi[i], t_lo[i], z_hi, z_lo)
        kept = lax.broadcasted_iota(jnp.int32, (8, rows.shape[1]), 0) < lead
        held[pl.ds(base, 8), :] = jnp.where(kept, held[pl.ds(base, 8), :], rows[:8])
        held[pl.ds(base + 8, CAP), :] = rows[8:CAP + 8]


def order_rows(counts, t_hi, t_lo, spread):
    width = spread.shape[2]
    group = 4
    factor = pl.BlockSpec((group, TALL, CAP), lambda s, counts: (s, 0, 0))
    return pl.pallas_call(
        order_kernel,
        grid_spec=pltpu.PrefetchScalarGridSpec(
            num_scalar_prefetch=1,
            grid=(16 // group,),
            in_specs=[factor, factor, pl.BlockSpec((group, CAP, width), lambda s, counts: (s, 0, 0))],
            out_specs=pl.BlockSpec((2048 + CAP + 8, width), lambda s, counts: (0, 0)),
        ),
        out_shape=jax.ShapeDtypeStruct((2048 + CAP + 8, width), jnp.float32),
    )(counts, t_hi, t_lo, spread)


def by_row_kernel(blocks, out, held, in_sem, out_sem):
    count, _, width = blocks.shape
    loads = [pltpu.make_async_copy(blocks.at[t], held.at[t], in_sem.at[t]) for t in range(count)]
    stores = [
        pltpu.make_async_copy(held.at[t], out.at[:, pl.ds(t * width, width)], out_sem.at[t]) for t in range(count)
    ]
    for load in loads:
        load.start()
    for load, store in zip(loads, stores):
        load.wait()
        store.start()
    for store in stores:
        store.wait()


def by_row(blocks):
    count, rows, width = blocks.shape
    return pl.pallas_call(
        by_row_kernel,
        out_shape=jax.ShapeDtypeStruct((rows, count * width), jnp.float32),
        in_specs=[pl.BlockSpec(memory_space=pl.ANY)],
        out_specs=pl.BlockSpec(memory_space=pl.ANY),
        scratch_shapes=[
            pltpu.VMEM(blocks.shape, jnp.float32), pltpu.SemaphoreType.DMA((count,)), pltpu.SemaphoreType.DMA((count,))
        ],
    )(blocks)


def body(raw_vectors, interval_count, cluster_of, panel_one, factor_one, panel_two, factor_two):
    spread, t_hi, t_lo, v_hi, v_lo, b_hi, b_lo = front(
        interval_count, raw_vectors, cluster_of, panel_one, factor_one, panel_two, factor_two
    )
    ordered = order_rows(interval_count, t_hi, t_lo, spread)
    return by_row(back_transform(ordered, v_hi, v_lo, b_hi, b_lo))


def solution(mesh):
    placed = (
        P("col", "row"),
        P(),
        P("col", None),
        P(("row", "col"), None),
        P(),
        P(("row", "col"), None),
        P(),
    )
    return jax.shard_map(
        body, mesh=mesh, in_specs=placed, out_specs=P("col", "row"), check_vma=False
    )
```
